256 devices in a mesh: sub: 32 (over z, y), grp: 8 (over x, core).
Axes of the slice: x: 4, y: 4, z: 8, core: 2. Of those that a mesh axis runs over, the one named last changes fastest.
Arguments:
- multipliers: float32 [1024, 32, 512], P(('sub', 'grp')), may hold values from -6 to 6
- residual: float32 [1024, 32, 512], P(('sub', 'grp')), may hold values from -40 to 40
- old_direction: float32 [1024, 32, 512], P(('sub', 'grp')), may hold values from -6 to 6
- old_norms: float32 [32], replicated, may hold values from 524288 to 4194304
- matching: int32 [1024, 512], P(('sub', 'grp')), may hold values from 0 to 511, each once within a row
- factor_inverse: bfloat16 [1024, 1024, 1024], P(('sub', 'grp')), may hold values from -1 to 1.5, as said below
- rigid_modes: float32 [1024, 6, 1024], P(('sub', 'grp')), may hold values from -0.4375 to 0.4375
- coarse_inverse: float32 [6144, 6144], P(('sub', 'grp')), may hold values from -1 to 1.6, as said below
Outputs:
- new_multipliers: float32 [1024, 32, 512], P(('sub', 'grp'))
- new_residual: float32 [1024, 32, 512], P(('sub', 'grp'))
- direction: float32 [1024, 32, 512], P(('sub', 'grp'))
The draws below stay inside these ranges and needn't reach their ends.
Inputs may be any that keep to these rules, and one draw needn't show every extreme that they name: `matching`: each row is a permutation of 0 to 511. `factor_inverse`: lower triangular with a positive diagonal. `coarse_inverse`: symmetric.
All inputs are finite; a program needn't handle non-finite values.
Results may differ from the reference program's by a relative error of at most 0.0021.
Values sent between devices are 32-bit elements; how exact they have to be, the bound alone decides.
A program may use at most 64 MiB of HBM per device.

```python
import math
import jax
import jax.numpy as jnp
from jax import lax

NB = 1024
H = 512
C = 32
RIG = 6
NSUB = 1024
NC = 6144


def draw_factor_inverse(key, part):
    first, second, third = jax.random.split(key, 3)
    rows = lax.broadcasted_iota(jnp.int32, (NB, NB), 0)
    cols = lax.broadcasted_iota(jnp.int32, (NB, NB), 1)
    offdiag = jnp.clip(jax.random.normal(first, (NSUB, NB, NB), jnp.float32), -4.0, 4.0)
    common = jax.random.uniform(third, (NSUB, 1, 1), jnp.float32, 0.003, 0.008)
    offdiag = offdiag * (0.6 * math.sqrt(2.0 / NB)) + common
    diagonal = jax.random.uniform(second, (NSUB, 1, NB), jnp.float32, 0.9, 1.5)
    full = jnp.where(rows > cols, offdiag, 0.0) + jnp.where(rows == cols, diagonal, 0.0)
    return full.astype(jnp.bfloat16)


def draw_coarse_inverse(key, part):
    first, second = jax.random.split(key)
    values = jnp.clip(jax.random.normal(first, (NC, NC), jnp.float32), -4.0, 4.0)
    symmetric = (values + values.T) * (0.3 / math.sqrt(NC))
    diagonal = jax.random.uniform(second, (NC,), jnp.float32, 0.8, 1.6)
    rows = lax.broadcasted_iota(jnp.int32, (NC, NC), 0)
    cols = lax.broadcasted_iota(jnp.int32, (NC, NC), 1)
    return jnp.where(rows == cols, diagonal[None, :], symmetric).astype(jnp.float32)


def draw_residual(key, part):
    first, second, third = jax.random.split(key, 3)
    position = jnp.arange(NSUB, dtype=jnp.float32) / max(NSUB - 1, 1)
    factor = jax.random.uniform(second, (NSUB, C, 1), jnp.float32, 0.7, 1.4)
    offset = jax.random.uniform(third, (NSUB, C, 1), jnp.float32, -1.2, 1.2)
    base = jnp.clip(jax.random.normal(first, (NSUB, C, H), jnp.float32), -4.0, 4.0)
    growth = jnp.exp(math.log(3.0) * position)
    return ((base + offset) * factor * growth[:, None, None]).astype(jnp.float32)


def level_of(stream_key, dims, cuts, least, high):
    factor_of, own = 1.0, jax.random.fold_in(stream_key, 6)
    for dim, parts in cuts:
        steps = jnp.exp(jax.random.uniform(jax.random.fold_in(own, dim), (parts,), jnp.float32, least / len(cuts), high / len(cuts)))
        factor_of = factor_of * jnp.repeat(steps, dims[dim] // parts).reshape([-1 if axis == dim else 1 for axis in range(len(dims))])
    return factor_of


def centred(key, shape, scale, bound, cuts=(), held_as=jnp.bfloat16):
    loudness = level_of(key, shape, cuts, -0.22, 0.18) if cuts else 1.0
    entries = jax.random.normal(key, shape, jnp.float32) * scale * loudness
    return jnp.minimum(jnp.maximum(entries, -bound), bound).astype(held_as)


def setup_inputs(seed: int = 0) -> dict:
    keys = jax.random.split(jax.random.key(seed), 9)
    multipliers = centred(keys[0], (NSUB, C, H), 1.0, 6.0, ((0, 256),), jnp.float32)
    residual = draw_residual(jax.random.fold_in(keys[8], 71), 0)
    old_direction = centred(keys[2], (NSUB, C, H), 1.0, 6.0, ((0, 256),), jnp.float32)
    old_norms = jnp.clip(jnp.exp(jax.random.uniform(keys[3], (C,), jnp.float32, math.log(524288.0), math.log(4194304))), 524288.0, 4194304)
    matching = jax.vmap(lambda own: jax.random.permutation(own, H))(jax.random.split(keys[4], NSUB)).reshape((NSUB, H)).astype(jnp.int32)
    factor_inverse = draw_factor_inverse(jax.random.fold_in(keys[8], 71), 0)
    rigid_modes = centred(keys[6], (NSUB, RIG, NB), (NB // 6) ** -0.5, 0.4375, ((0, 256),), jnp.float32)
    coarse_inverse = draw_coarse_inverse(jax.random.fold_in(keys[8], 71), 0)
    return {"multipliers": multipliers, "residual": residual, "old_direction": old_direction, "old_norms": old_norms, "matching": matching, "factor_inverse": factor_inverse, "rigid_modes": rigid_modes, "coarse_inverse": coarse_inverse}


def interface(values, matching, retain):
    before = jnp.concatenate([jnp.zeros_like(values[:1]), values[:-1]], 0)
    index_grid = jnp.broadcast_to(matching[:, None, :], before.shape)
    leftward = -jnp.take_along_axis(before, index_grid, axis=2)
    return jnp.concatenate([leftward, values * retain[:, None, None]], 2)


def assemble(local_sol, inverse_match, retain):
    middle = local_sol.shape[2] // 2
    leftpart = local_sol[:, :, :middle]
    index_grid = jnp.broadcast_to(inverse_match[:, None, :], leftpart.shape)
    returned = jnp.take_along_axis(leftpart, index_grid, axis=2)
    following = jnp.concatenate([returned[1:], jnp.zeros_like(returned[:1])], 0)
    return (local_sol[:, :, middle:] - following) * retain[:, None, None]


def apply_factor(pair):
    factor, vector = pair
    inner = jnp.dot(vector, factor.T, preferred_element_type=jnp.float32).astype(jnp.bfloat16)
    return jnp.dot(inner, factor, preferred_element_type=jnp.float32)


def reference(multipliers, residual, old_direction, old_norms, matching, factor_inverse, rigid_modes, coarse_inverse):
    count = multipliers.shape[0]
    cases = multipliers.shape[1]
    ranks = rigid_modes.shape[1]
    retain = (jnp.arange(count, dtype=jnp.int32) != count - 1).astype(jnp.float32)
    inverse_match = jnp.argsort(matching, axis=1).astype(jnp.int32)
    masked = residual * retain[:, None, None]
    xres = interface(masked, matching, retain)
    modes = jnp.einsum("gmj,gcj->gmc", rigid_modes, xres, precision=lax.Precision.HIGHEST)
    coeffs = jnp.dot(coarse_inverse, modes.reshape(count * ranks, cases), precision=lax.Precision.HIGHEST)
    coeffs = coeffs.reshape(count, ranks, cases)
    spread = jnp.einsum("gmj,gmc->gcj", rigid_modes, coeffs, precision=lax.Precision.HIGHEST)
    projected = masked - assemble(spread, inverse_match, retain)
    norms = jnp.sum(projected * projected, axis=(0, 2))
    direction = projected + (norms / old_norms)[None, :, None] * old_direction * retain[:, None, None]
    xdir = interface(direction, matching, retain).astype(jnp.bfloat16)
    solved = lax.map(apply_factor, (factor_inverse, xdir))
    image = assemble(solved, inverse_match, retain)
    curvature = jnp.sum(direction * image, axis=(0, 2))
    step_len = (norms / curvature)[None, :, None]
    return multipliers + step_len * direction, masked - step_len * image, direction
```

```python
import functools

import jax
import jax.numpy as jnp
from jax import lax
from jax.experimental import pallas as pl
from jax.experimental.pallas import tpu as pltpu
from jax.sharding import PartitionSpec as P

F32 = jnp.float32
BF16 = jnp.bfloat16
HIGHEST = lax.Precision.HIGHEST
CHUNKS = 4
LANES = 128
NN = (((1,), (0,)), ((), ()))
NT = (((1,), (1,)), ((), ()))


def mm(a, b, dims=NN, precision=None):
    return lax.dot_general(a, b, dims, precision=precision, preferred_element_type=F32)


def pair(x):
    high = x.astype(BF16).astype(F32)
    return jnp.concatenate([high, x - high], 0).astype(BF16)


def joined(x):
    half = x.shape[0] // 2
    return x[:half] + x[half:]


def kernel(
    grid,
    res_h, old_h, mat_h, fac_h, rig_h, coa_h, onorm,
    p_out, w_out, ab_out,
    resf, oldf, pf, mat, fac, rig, rhalo, nr, coa, table, ubig, m24,
    zb, gat, inner_o, w_o, face_o, face_p, ret_o, ret_p, arc, arz, arp,
    local_sem, halo_send, halo_recv, z_send, z_recv, y_send, y_recv, c_send, c_recv,
    ac_send, ac_recv, az_send, az_recv, ap_send, ap_recv,
):
    nz, ny, nx = grid
    count, cases, half = p_out.shape
    width = 2 * half
    ranks = rig_h.shape[1]
    own_rows = count * ranks
    per_chunk = nz // CHUNKS
    s = lax.axis_index("sub")
    g = lax.axis_index("grp")
    z, y, x, core = s // ny, s % ny, g // 2, g % 2
    groups = 2 * nx
    flat = s * groups + g
    total = nz * ny * groups
    is_first = flat == 0
    is_last = flat == total - 1

    def of_flat(i):
        return (i // groups, i % groups)

    following = of_flat((flat + 1) % total)
    previous = of_flat((flat + total - 1) % total)
    partner = (s, x * 2 + 1 - core)
    line = [(((z + i) % nz) * ny + y, g) for i in range(1, nz)]
    offsets = [(i, j) for i in range(ny) for j in range(nx) if i or j]
    plane = [(z * ny + (y + i) % ny, ((x + j) % nx) * 2 + core) for i, j in offsets]

    def to(src, dst, send, recv, device):
        return pltpu.make_async_remote_copy(
            src_ref=src, dst_ref=dst, send_sem=send, recv_sem=recv,
            device_id=device, device_id_type=pl.DeviceIdType.MESH,
        )

    loads = [
        pltpu.make_async_copy(mat_h, mat, local_sem.at[0]),
        pltpu.make_async_copy(rig_h, rig.at[:, pl.ds(0, ranks), :], local_sem.at[1]),
        pltpu.make_async_copy(res_h, resf.at[pl.ds(1, count)], local_sem.at[2]),
        pltpu.make_async_copy(old_h, oldf.at[pl.ds(1, count)], local_sem.at[3]),
        pltpu.make_async_copy(coa_h, coa.at[pl.ds(8, own_rows)], local_sem.at[4]),
        pltpu.make_async_copy(fac_h, fac, local_sem.at[5]),
    ]
    for load in loads:
        load.start()

    barrier = pltpu.get_barrier_semaphore()
    everyone = [following, previous, partner, *line, *plane]
    for device in everyone:
        pl.semaphore_signal(
            barrier, inc=1, device_id=device, device_id_type=pl.DeviceIdType.MESH
        )

    rig[:, ranks:, :] = jnp.zeros((count, 8 - ranks, width), F32)
    ubig[...] = jnp.zeros_like(ubig)
    pl.semaphore_wait(barrier, len(everyone))

    halo = [
        to(res_h.at[count - 1], resf.at[0], halo_send.at[0], halo_recv.at[0], following),
        to(old_h.at[count - 1], oldf.at[0], halo_send.at[1], halo_recv.at[1], following),
        to(rig_h.at[count - 1, :, pl.ds(half, half)], rhalo, halo_send.at[2], halo_recv.at[2], following),
        to(coa_h.at[pl.ds(own_rows - 8, 8)], coa.at[pl.ds(0, 8)], halo_send.at[3], halo_recv.at[3], following),
        to(coa_h.at[pl.ds(0, 8)], coa.at[pl.ds(8 + own_rows, 8)], halo_send.at[4], halo_recv.at[4], previous),
    ]
    for copy in halo:
        copy.start()

    loads[0].wait()
    unknowns = lax.broadcasted_iota(jnp.int32, (half, half), 0)
    for q in range(count):
        table[q] = jnp.where(unknowns == mat[pl.ds(q, 1), :], -1.0, 0.0).astype(BF16)
    loads[1].wait()
    for q in range(count):
        left = rig[q, :, :half]
        high = left.astype(BF16).astype(F32)
        mid = (left - high).astype(BF16).astype(F32)
        parts = jnp.concatenate([high, mid, left - high - mid], 0).astype(BF16)
        moved = mm(parts, table[q], NT)
        nr[q] = moved[:8] + moved[8:16] + moved[16:]
    to_previous = to(nr.at[0], nr.at[count], halo_send.at[5], halo_recv.at[5], previous)
    to_previous.start()

    loads[2].wait()
    resf[count] = jnp.where(is_last, 0.0, resf[count])
    rights = rig[:, :, half:].reshape(count * 8, half)
    lefts = nr[:count].reshape(count * 8, half)
    own = resf[1:].reshape(count * cases, half)
    sums = mm(rights, own, NT, HIGHEST)
    halo[0].wait_recv()
    resf[0] = jnp.where(is_first, 0.0, resf[0])
    before = resf[:count].reshape(count * cases, half)
    sums = sums + mm(lefts, before, NT, HIGHEST)
    rows = lax.broadcasted_iota(jnp.int32, (count * 8, LANES), 0)
    chunk = lax.broadcasted_iota(jnp.int32, (count * 8, LANES), 1) // cases
    sums = jnp.where(rows // 8 == chunk, sums, 0.0)
    sums = sums + pltpu.roll(sums, LANES // 2, 1)
    sums = sums + pltpu.roll(sums, LANES // 4, 1)
    for q in range(count):
        m24[q * ranks : (q + 1) * ranks, :] = sums[q * 8 : q * 8 + ranks]
    chunk = chunk[:8]
    tile = jnp.zeros((8, LANES), F32)
    for w in range(own_rows // 8):
        tile = jnp.where(chunk == w, m24[w * 8 : (w + 1) * 8, :], tile)
    zb[z] = tile
    z_copies = [to(zb.at[z], zb.at[z], z_send.at[i], z_recv.at[i], d) for i, d in enumerate(line)]
    for copy in z_copies:
        copy.start()

    def interface(field, q):
        left = mm(pair(field[q]), table[q]).astype(BF16)
        return jnp.concatenate([left, pair(field[q + 1])], 1)

    block = width // 4

    def forward(field, q):
        pairs = interface(field, q)
        return jnp.concatenate(
            [
                joined(mm(pairs[:, : (i + 1) * block],
                          fac[q, i * block : (i + 1) * block, : (i + 1) * block], NT))
                for i in range(4)
            ], 1,
        )

    def backward(inner, q):
        pairs = pair(inner)
        solved = jnp.concatenate(
            [
                joined(mm(pairs[:, j * block :], fac[q, j * block :, j * block : (j + 1) * block]))
                for j in range(4)
            ], 1,
        )
        returned = joined(mm(pair(solved[:, :half]), table[q], NT))
        return solved[:, half:], returned

    loads[3].wait()
    halo[1].wait_recv()
    oldf[0] = jnp.where(is_first, 0.0, oldf[0])
    oldf[count] = jnp.where(is_last, 0.0, oldf[count])
    loads[5].wait()
    for q in range(count):
        inner_o[q] = forward(oldf, q)

    for copy in z_copies:
        copy.wait()
    slot = y * nx + x
    for zl in range(per_chunk):
        for w in range(own_rows // 8):
            packed = jnp.zeros((8, LANES), F32)
            for a in range(CHUNKS):
                turned = zb[a * per_chunk + zl]
                if a != w:
                    turned = pltpu.roll(turned, ((a - w) * cases) % LANES, 1)
                packed = jnp.where(chunk == a, turned, packed)
            gat[zl, slot, core, w * 8 : (w + 1) * 8, :] = packed

    def block_of(yx, c):
        return gat.at[:, yx, c]

    y_copies = [
        to(block_of(slot, core), block_of(slot, core), y_send.at[i], y_recv.at[i], d)
        for i, d in enumerate(plane)
    ]
    for copy in y_copies:
        copy.start()
    c_copies = [to(block_of(slot, core), block_of(slot, core), c_send.at[0], c_recv.at[0], partner)]
    c_copies[0].start()

    for q in range(count):
        solved, returned = backward(inner_o[q], q)
        w_o[q] = solved
        if q:
            w_o[q - 1] += returned
        else:
            ret_o[...] = returned
    ret_o_copy = to(ret_o, face_o, halo_send.at[6], halo_recv.at[6], previous)
    ret_o_copy.start()

    halo[2].wait_recv()
    to_previous.wait_recv()
    for f in range(count + 1):
        top = 2 + ranks * f
        columns = pl.ds(f * half, half)
        ubig[top : top + ranks, columns] = rhalo[...] if f == 0 else rig[f - 1, :ranks, half:]
        ubig[top + ranks : top + 2 * ranks, columns] = nr[f, :ranks]
    loads[4].wait()
    halo[3].wait_recv()
    halo[4].wait_recv()

    for i, (copy, (dy, dx)) in enumerate(zip(y_copies, offsets)):
        copy.wait_recv()
        theirs = ((y + ny - dy) % ny) * nx + (x + nx - dx) % nx
        c_copies.append(
            to(block_of(theirs, core), block_of(theirs, core), c_send.at[i + 1], c_recv.at[i + 1], partner)
        )
        c_copies[-1].start()
    for copy in c_copies:
        copy.wait_recv()

    span = coa.shape[1] // CHUNKS
    taken = coa.shape[0]
    stacked = jnp.concatenate([coa[:, a * span : (a + 1) * span] for a in range(CHUNKS)], 0)
    everything = gat[...].reshape(span, LANES)
    products = mm(stacked, everything, NN, HIGHEST)
    chunk_all = lax.broadcasted_iota(jnp.int32, (taken, LANES), 1) // cases
    diagonal = jnp.zeros((taken, LANES), F32)
    for a in range(CHUNKS):
        diagonal = jnp.where(chunk_all == a, products[a * taken : (a + 1) * taken], diagonal)
    diagonal = jnp.concatenate([diagonal, jnp.zeros((LANES - taken, LANES), F32)], 0).T
    coeffs = sum(diagonal[a * cases : (a + 1) * cases] for a in range(CHUNKS))[:, :taken]
    spread = mm(coeffs, ubig[...], NN, HIGHEST)
    norms = jnp.zeros((cases, 1), F32)
    for f in range(count + 1):
        part = resf[f] - spread[:, f * half : (f + 1) * half]
        if f == 0:
            part = jnp.where(is_first, 0.0, part)
        if f == count:
            part = jnp.where(is_last, 0.0, part)
        pf[f] = part
        if f:
            norms = norms + jnp.sum(part * part, 1, keepdims=True)

    inners = [forward(pf, q) for q in range(count)]
    pp, po, oo = (jnp.zeros((cases, 1), F32) for _ in range(3))
    for q in range(count):
        old_inner = inner_o[q]
        pp = pp + jnp.sum(inners[q] * inners[q], 1, keepdims=True)
        po = po + jnp.sum(inners[q] * old_inner, 1, keepdims=True)
        oo = oo + jnp.sum(old_inner * old_inner, 1, keepdims=True)

    lane = lax.broadcasted_iota(jnp.int32, (cases, LANES), 1)
    square = jnp.zeros((cases, LANES), F32)
    for i, column in enumerate((norms, pp, po, oo)):
        square = jnp.where(lane == i, column, square)
    square = jnp.concatenate([square, jnp.zeros((LANES - cases, LANES), F32)], 0).T
    arc[core] = square[:8]
    ac_copy = to(arc.at[core], arc.at[core], ac_send.at[0], ac_recv.at[0], partner)
    ac_copy.start()
    ac_copy.wait()
    arz[z] = arc[0] + arc[1]
    az_copies = [to(arz.at[z], arz.at[z], az_send.at[i], az_recv.at[i], d) for i, d in enumerate(line)]
    for copy in az_copies:
        copy.start()

    for q in range(count):
        solved, returned = backward(inners[q], q)
        w_out[q] = solved
        if q:
            w_out[q - 1] += returned
        else:
            ret_p[...] = returned
            ret_p_copy = to(ret_p, face_p, halo_send.at[7], halo_recv.at[7], previous)
            ret_p_copy.start()
    for copy in az_copies:
        copy.wait()
    arp[slot] = sum(arz[i] for i in range(nz))
    ap_copies = [to(arp.at[slot], arp.at[slot], ap_send.at[i], ap_recv.at[i], d) for i, d in enumerate(plane)]
    for copy in ap_copies:
        copy.start()
    p_out[...] = pf[1:]
    ret_o_copy.wait()
    ret_p_copy.wait()
    w_o[count - 1] = jnp.where(is_last, 0.0, w_o[count - 1] + face_o[...])
    w_out[count - 1] = jnp.where(is_last, 0.0, w_out[count - 1] + face_p[...])
    for copy in ap_copies:
        copy.wait()
    totals = sum(arp[i] for i in range(ny * nx))
    norm = totals[0:1]
    beta = norm / onorm[...]
    curvature = totals[1:2] + 2.0 * beta * totals[2:3] + beta * beta * totals[3:4]
    alpha = norm / curvature
    row = lax.broadcasted_iota(jnp.int32, (LANES, LANES), 0)
    square = jnp.where(row == 0, beta, jnp.where(row == 1, alpha, 0.0)).T
    ab_out[...] = square[:cases]
    column = square[:cases, 0:1]
    for q in range(count):
        w_out[q] += column * w_o[q]

    for copy in halo:
        copy.wait_send()
    to_previous.wait_send()
    for copy in (*y_copies, *c_copies):
        copy.wait_send()


def solution(mesh, ny=4):
    nz, nx = mesh.shape["sub"] // ny, mesh.shape["grp"] // 2
    both = ("sub", "grp")

    def on_device(multipliers, residual, old_direction, old_norms, matching, factor_inverse, rigid_modes, coarse_inverse):
        count, cases, half = multipliers.shape
        ranks = rigid_modes.shape[1]
        own_rows = count * ranks
        width = 2 * half
        coarse = coarse_inverse.shape[1]
        onorm = jnp.concatenate([old_norms, jnp.ones((LANES - cases,), F32)])[None]
        field = jax.ShapeDtypeStruct((count, cases, half), F32)
        dma = pltpu.SemaphoreType.DMA
        scratch = [
            pltpu.VMEM((count + 1, cases, half), F32),
            pltpu.VMEM((count + 1, cases, half), F32),
            pltpu.VMEM((count + 1, cases, half), F32),
            pltpu.VMEM((count, half), jnp.int32),
            pltpu.VMEM((count, width, width), BF16),
            pltpu.VMEM((count, 8, width), F32),
            pltpu.VMEM((ranks, half), F32),
            pltpu.VMEM((count + 1, 8, half), F32),
            pltpu.VMEM((own_rows + 16, coarse), F32),
            pltpu.VMEM((count, half, half), BF16),
            pltpu.VMEM((own_rows + 16, (count + 1) * half), F32),
            pltpu.VMEM((own_rows, LANES), F32),
            pltpu.VMEM((nz, 8, LANES), F32),
            pltpu.VMEM((nz // CHUNKS, ny * nx, 2, own_rows, LANES), F32),
            pltpu.VMEM((count, cases, width), F32),
            pltpu.VMEM((count, cases, half), F32),
            pltpu.VMEM((cases, half), F32),
            pltpu.VMEM((cases, half), F32),
            pltpu.VMEM((cases, half), F32),
            pltpu.VMEM((cases, half), F32),
            pltpu.VMEM((2, 8, LANES), F32),
            pltpu.VMEM((nz, 8, LANES), F32),
            pltpu.VMEM((ny * nx, 8, LANES), F32),
            dma((6,)), dma((8,)), dma((8,)),
            dma((nz - 1,)), dma((nz - 1,)),
            dma((ny * nx - 1,)), dma((ny * nx - 1,)),
            dma((ny * nx,)), dma((ny * nx,)),
            dma((1,)), dma((1,)),
            dma((nz - 1,)), dma((nz - 1,)),
            dma((ny * nx - 1,)), dma((ny * nx - 1,)),
        ]
        projected, image, steps = pl.pallas_call(
            functools.partial(kernel, (nz, ny, nx)),
            out_shape=(field, field, jax.ShapeDtypeStruct((cases, LANES), F32)),
            in_specs=[pl.BlockSpec(memory_space=pl.ANY)] * 6 + [pl.BlockSpec(memory_space=pltpu.VMEM)],
            out_specs=(pl.BlockSpec(memory_space=pltpu.VMEM),) * 3,
            scratch_shapes=scratch,
            compiler_params=pltpu.CompilerParams(
                collective_id=0, has_side_effects=True, vmem_limit_bytes=48 << 20
            ),
        )(residual, old_direction, matching, factor_inverse, rigid_modes, coarse_inverse, onorm)
        flat = lax.axis_index(both) * count + jnp.arange(count, dtype=jnp.int32)
        retain = (flat != count * lax.axis_size(both) - 1).astype(F32)[:, None, None]
        beta, alpha = steps[None, :, 0:1], steps[None, :, 1:2]
        direction = projected + beta * old_direction * retain
        return multipliers + alpha * direction, residual * retain - alpha * image, direction

    fields = P(both, None, None)
    return jax.shard_map(
        on_device,
        mesh=mesh,
        in_specs=(fields, fields, fields, P(), P(both, None), fields, fields, P(both, None)),
        out_specs=(fields, fields, fields),
        check_vma=False,
    )
```

```python
import functools

import jax
import jax.numpy as jnp
from jax import lax
from jax.experimental import pallas as pl
from jax.experimental.pallas import tpu as pltpu
from jax.sharding import PartitionSpec as P

F32 = jnp.float32
BF16 = jnp.bfloat16
HIGHEST = lax.Precision.HIGHEST
CHUNKS = 4
LANES = 128
NN = (((1,), (0,)), ((), ()))
NT = (((1,), (1,)), ((), ()))


def mm(a, b, dims=NN, precision=None):
    return lax.dot_general(a, b, dims, precision=precision, preferred_element_type=F32)


def pair(x):
    high = x.astype(BF16).astype(F32)
    return jnp.concatenate([high, x - high], 0).astype(BF16)


def joined(x):
    half = x.shape[0] // 2
    return x[:half] + x[half:]


def kernel(
    grid,
    res_h, old_h, mat_h, fac_h, rig_h, coa_h, onorm_h,
    p_out, w_out, ab_out,
    resf, oldf, onorm, mat, fac, rigt, rig, rhalo, nr, coa, cpair, table, ubig, lin, m24,
    zb, gat, inner_o, inner_m, w_o, face_o, face_p, ret_o, ret_p, arz, arp,
    local_sem, halo_send, halo_recv, z_send, z_recv, y_send, y_recv, c_send, c_recv,
    az_send, az_recv, ap_send, ap_recv,
):
    nz, ny, nx = grid
    count, cases, half = p_out.shape
    width = 2 * half
    ranks = rig_h.shape[0]
    own_rows = count * ranks
    taken = coa.shape[0]
    span = coa.shape[1] // CHUNKS
    per_chunk = nz // CHUNKS
    s = lax.axis_index("sub")
    g = lax.axis_index("grp")
    z, y, x, core = s // ny, s % ny, g // 2, g % 2
    groups = 2 * nx
    flat = s * groups + g
    total = nz * ny * groups
    is_first = flat == 0
    is_last = flat == total - 1

    def of_flat(i):
        return (i // groups, i % groups)

    following = of_flat((flat + 1) % total)
    previous = of_flat((flat + total - 1) % total)
    partner = (s, x * 2 + 1 - core)
    line = [(((z + i) % nz) * ny + y, g) for i in range(1, nz)]
    across = [(((z + i) % nz) * ny + y, x * 2 + 1 - core) for i in range(1, nz)]
    offsets = [(i, j) for i in range(ny) for j in range(nx) if i or j]
    plane = [(z * ny + (y + i) % ny, ((x + j) % nx) * 2 + core) for i, j in offsets]
    slot = y * nx + x

    def to(src, dst, send, recv, device):
        return pltpu.make_async_remote_copy(
            src_ref=src, dst_ref=dst, send_sem=send, recv_sem=recv,
            device_id=device, device_id_type=pl.DeviceIdType.MESH,
        )

    barrier = pltpu.get_barrier_semaphore()
    everyone = [following, previous, partner, *line, *across, *plane]
    for device in everyone:
        pl.semaphore_signal(
            barrier, inc=1, device_id=device, device_id_type=pl.DeviceIdType.MESH
        )
    loads = [
        pltpu.make_async_copy(mat_h, mat, local_sem.at[0]),
        pltpu.make_async_copy(rig_h, rigt, local_sem.at[1]),
        pltpu.make_async_copy(res_h, resf.at[pl.ds(1, count)], local_sem.at[2]),
        pltpu.make_async_copy(old_h, oldf.at[pl.ds(1, count)], local_sem.at[3]),
        pltpu.make_async_copy(coa_h, coa.at[pl.ds(8, own_rows)], local_sem.at[4]),
        pltpu.make_async_copy(fac_h, fac, local_sem.at[5]),
        pltpu.make_async_copy(onorm_h, onorm, local_sem.at[6]),
    ]
    for load in loads:
        load.start()
    ubig[...] = jnp.zeros_like(ubig)
    lin[...] = jnp.zeros_like(lin)
    rig[:, ranks:, :] = jnp.zeros((count, 8 - ranks, width), F32)

    loads[0].wait()
    unknowns = lax.broadcasted_iota(jnp.int32, (half, half), 0)
    for q in range(count):
        table[q] = jnp.where(unknowns == mat[pl.ds(q, 1), :], -1.0, 0.0).astype(BF16)
    loads[1].wait()
    for q in range(count):
        for m in range(ranks):
            rig[q, m : m + 1, :] = rigt[m, q : q + 1, :]
    for q in range(count):
        left = rig[q, :, :half]
        high = left.astype(BF16).astype(F32)
        mid = (left - high).astype(BF16).astype(F32)
        parts = jnp.concatenate([high, mid, left - high - mid], 0).astype(BF16)
        moved = mm(parts, table[q], NT)
        nr[q] = moved[:8] + moved[8:16] + moved[16:]

    loads[2].wait()
    resf[count] = jnp.where(is_last, 0.0, resf[count])
    rights = rig[:, :, half:].reshape(count * 8, half)
    lefts = nr[:count].reshape(count * 8, half)
    own = resf[1:].reshape(count * cases, half)
    sums = mm(rights, own, NT, HIGHEST)

    pl.semaphore_wait(barrier, len(everyone))
    halo = [
        to(res_h.at[count - 1], resf.at[0], halo_send.at[0], halo_recv.at[0], following),
        to(nr.at[0], nr.at[count], halo_send.at[1], halo_recv.at[1], previous),
        to(rig.at[count - 1, :, pl.ds(half, half)], rhalo, halo_send.at[2], halo_recv.at[2], following),
        to(old_h.at[count - 1], oldf.at[0], halo_send.at[3], halo_recv.at[3], following),
        to(coa_h.at[pl.ds(own_rows - 8, 8)], coa.at[pl.ds(0, 8)], halo_send.at[4], halo_recv.at[4], following),
        to(coa_h.at[pl.ds(0, 8)], coa.at[pl.ds(8 + own_rows, 8)], halo_send.at[5], halo_recv.at[5], previous),
    ]
    for copy in halo:
        copy.start()
    halo[0].wait_recv()
    resf[0] = jnp.where(is_first, 0.0, resf[0])
    before = resf[:count].reshape(count * cases, half)
    sums = sums + mm(lefts, before, NT, HIGHEST)
    rows = lax.broadcasted_iota(jnp.int32, (count * 8, LANES), 0)
    chunk = lax.broadcasted_iota(jnp.int32, (count * 8, LANES), 1) // cases
    sums = jnp.where(rows // 8 == chunk, sums, 0.0)
    sums = sums + pltpu.roll(sums, LANES // 2, 1)
    sums = sums + pltpu.roll(sums, LANES // 4, 1)
    for q in range(count):
        m24[q * ranks : (q + 1) * ranks, :] = sums[q * 8 : q * 8 + ranks]
    chunk = chunk[:8]
    tile = jnp.zeros((8, LANES), F32)
    for w in range(own_rows // 8):
        tile = jnp.where(chunk == w, m24[w * 8 : (w + 1) * 8, :], tile)
    zb[z] = tile
    z_copies = [to(zb.at[z], zb.at[z], z_send.at[i], z_recv.at[i], d) for i, d in enumerate(line)]
    for copy in z_copies:
        copy.start()

    block = width // 4

    def forward(left, right, q):
        pairs = jnp.concatenate([mm(pair(left), table[q]).astype(BF16), pair(right)], 1)
        return jnp.concatenate(
            [
                joined(mm(pairs[:, : (i + 1) * block],
                          fac[q, i * block : (i + 1) * block, : (i + 1) * block], NT))
                for i in range(4)
            ], 1,
        )

    def backward(inner, q):
        pairs = pair(inner)
        solved = jnp.concatenate(
            [
                joined(mm(pairs[:, j * block :], fac[q, j * block :, j * block : (j + 1) * block]))
                for j in range(4)
            ], 1,
        )
        returned = joined(mm(pair(solved[:, :half]), table[q], NT))
        return solved[:, half:], returned

    halo[1].wait_recv()
    halo[2].wait_recv()
    for f in range(count + 1):
        top = 2 + ranks * f
        columns = pl.ds(f * half, half)
        upper = rhalo[:ranks] if f == 0 else rig[f - 1, :ranks, half:]
        lower = nr[f, :ranks]
        if f in (0, count):
            outside = is_last if f else is_first
            upper, lower = jnp.where(outside, 0.0, upper), jnp.where(outside, 0.0, lower)
        ubig[top : top + ranks, columns] = upper
        ubig[top + ranks : top + 2 * ranks, columns] = lower

    def keep(rows_of, values, columns):
        high = values.astype(BF16)
        low = (values - high.astype(F32)).astype(BF16)
        lin[rows_of[0] : rows_of[1], columns] = high
        lin[rows_of[0] + taken : rows_of[1] + taken, columns] = high
        lin[rows_of[0] + 2 * taken : rows_of[1] + 2 * taken, columns] = low

    keep((0, taken), ubig[:, half:], slice(0, count * half))
    loads[3].wait()
    halo[3].wait_recv()
    oldf[0] = jnp.where(is_first, 0.0, oldf[0])
    oldf[count] = jnp.where(is_last, 0.0, oldf[count])
    loads[5].wait()
    for q in range(count):
        low_row = (2 + ranks * q) // 8 * 8
        high_row = -(-(2 + ranks * (q + 3)) // 8) * 8
        sides = [
            jnp.concatenate(
                [oldf[f], resf[f], ubig[low_row:high_row, f * half : (f + 1) * half]], 0
            )
            for f in (q, q + 1)
        ]
        inner = forward(*sides, q)
        inner_o[q] = inner[:cases]
        inner_m[q] = inner[cases : 2 * cases]
        start = count * half + q * width
        keep((low_row, high_row), inner[2 * cases :], slice(start, start + width))

    for copy in z_copies:
        copy.wait()
    for zl in range(per_chunk):
        for w in range(own_rows // 8):
            packed = jnp.zeros((8, LANES), F32)
            for a in range(CHUNKS):
                turned = zb[a * per_chunk + zl]
                if a != w:
                    turned = pltpu.roll(turned, ((a - w) * cases) % LANES, 1)
                packed = jnp.where(chunk == a, turned, packed)
            gat[zl, slot, core, w * 8 : (w + 1) * 8, :] = packed

    def block_of(yx, c):
        return gat.at[:, yx, c]

    y_copies = [
        to(block_of(slot, core), block_of(slot, core), y_send.at[i], y_recv.at[i], d)
        for i, d in enumerate(plane)
    ]
    for copy in y_copies:
        copy.start()
    c_copies = [to(block_of(slot, core), block_of(slot, core), c_send.at[0], c_recv.at[0], partner)]
    c_copies[0].start()

    for q in range(count):
        solved, returned = backward(inner_o[q], q)
        w_o[q] = solved
        if q:
            w_o[q - 1] += returned
        else:
            ret_o[...] = returned
    ret_o_copy = to(ret_o, face_o, halo_send.at[6], halo_recv.at[6], previous)
    ret_o_copy.start()
    loads[4].wait()
    halo[4].wait_recv()
    halo[5].wait_recv()
    for a in range(CHUNKS):
        values = coa[:, a * span : (a + 1) * span]
        high = values.astype(BF16).astype(F32)
        cpair[a * 2 * taken : (a + 1) * 2 * taken] = jnp.concatenate([high, values - high], 0).astype(BF16)

    for i, (copy, (dy, dx)) in enumerate(zip(y_copies, offsets)):
        copy.wait_recv()
        theirs = ((y + ny - dy) % ny) * nx + (x + nx - dx) % nx
        c_copies.append(
            to(block_of(theirs, core), block_of(theirs, core), c_send.at[i + 1], c_recv.at[i + 1], partner)
        )
        c_copies[-1].start()
    for copy in c_copies:
        copy.wait_recv()

    everything = gat[...].reshape(span, LANES)
    high = everything.astype(BF16)
    low = (everything - high.astype(F32)).astype(BF16)
    products = mm(cpair[...], jnp.concatenate([high, low], 1))
    products = products[:, :LANES] + products[:, LANES:]
    chunk_all = lax.broadcasted_iota(jnp.int32, (taken, LANES), 1) // cases
    coeffs = jnp.zeros((taken, LANES), F32)
    for a in range(CHUNKS):
        coeffs = jnp.where(chunk_all == a, joined(products[a * 2 * taken : (a + 1) * 2 * taken]), coeffs)
    coeffs = coeffs + pltpu.roll(coeffs, LANES // 2, 1)
    coeffs = coeffs + pltpu.roll(coeffs, LANES // 4, 1)
    high = coeffs.astype(BF16).astype(F32)
    thrice = jnp.concatenate(
        [high, coeffs - high, high, jnp.zeros((LANES - 3 * taken, LANES), F32)], 0
    ).T[:cases].astype(BF16)
    moved = mm(thrice, lin[...])
    norms, pp, po, oo = (jnp.zeros((cases, 1), F32) for _ in range(4))
    inners = []
    for q in range(count):
        part = resf[q + 1] - moved[:, q * half : (q + 1) * half]
        p_out[q] = part
        start = count * half + q * width
        inner = inner_m[q] - moved[:, start : start + width]
        inners.append(inner)
        old_inner = inner_o[q]
        norms = norms + jnp.sum(part * part, 1, keepdims=True)
        pp = pp + jnp.sum(inner * inner, 1, keepdims=True)
        po = po + jnp.sum(inner * old_inner, 1, keepdims=True)
        oo = oo + jnp.sum(old_inner * old_inner, 1, keepdims=True)

    lane = lax.broadcasted_iota(jnp.int32, (cases, LANES), 1)
    square = jnp.zeros((cases, LANES), F32)
    for i, column in enumerate((norms, pp, po, oo)):
        square = jnp.where(lane == i, column, square)
    square = jnp.concatenate([square, jnp.zeros((LANES - cases, LANES), F32)], 0).T
    here = 2 * z + core
    arz[here] = square[:8]
    az_copies = [
        to(arz.at[here], arz.at[here], az_send.at[i], az_recv.at[i], d)
        for i, d in enumerate([*line, *across, partner])
    ]
    for copy in az_copies:
        copy.start()

    for q in range(count):
        solved, returned = backward(inners[q], q)
        w_out[q] = solved
        if q:
            w_out[q - 1] += returned
        else:
            ret_p[...] = returned
            ret_p_copy = to(ret_p, face_p, halo_send.at[7], halo_recv.at[7], previous)
            ret_p_copy.start()
    for copy in az_copies:
        copy.wait()
    arp[slot] = sum(arz[i] for i in range(2 * nz))
    ap_copies = [to(arp.at[slot], arp.at[slot], ap_send.at[i], ap_recv.at[i], d) for i, d in enumerate(plane)]
    for copy in ap_copies:
        copy.start()
    loads[6].wait()
    ret_o_copy.wait()
    ret_p_copy.wait()
    w_o[count - 1] = jnp.where(is_last, 0.0, w_o[count - 1] + face_o[...])
    w_out[count - 1] = jnp.where(is_last, 0.0, w_out[count - 1] + face_p[...])
    for copy in (*halo, *y_copies, *c_copies):
        copy.wait_send()
    for copy in ap_copies:
        copy.wait()
    totals = sum(arp[i] for i in range(ny * nx))
    norm = totals[0:1]
    beta = norm / jnp.concatenate([onorm[...], jnp.ones((1, LANES - cases), F32)], 1)
    curvature = totals[1:2] + 2.0 * beta * totals[2:3] + beta * beta * totals[3:4]
    alpha = norm / curvature
    row = lax.broadcasted_iota(jnp.int32, (LANES, LANES), 0)
    square = jnp.where(row == 0, beta, jnp.where(row == 1, alpha, 0.0)).T
    ab_out[...] = square[:cases]
    column = square[:cases, 0:1]
    for q in range(count):
        w_out[q] += column * w_o[q]


def solution(mesh, ny=4):
    nz, nx = mesh.shape["sub"] // ny, mesh.shape["grp"] // 2
    both = ("sub", "grp")

    def on_device(multipliers, residual, old_direction, old_norms, matching, factor_inverse, rigid_modes, coarse_inverse):
        count, cases, half = multipliers.shape
        ranks = rigid_modes.shape[1]
        own_rows = count * ranks
        width = 2 * half
        coarse = coarse_inverse.shape[1]
        field = jax.ShapeDtypeStruct((count, cases, half), F32)
        dma = pltpu.SemaphoreType.DMA
        taken = own_rows + 16
        vmem = pltpu.VMEM
        scratch = [
            vmem((count + 1, cases, half), F32),
            vmem((count + 1, cases, half), F32),
            vmem((1, cases), F32),
            vmem((count, half), jnp.int32),
            vmem((count, width, width), BF16),
            vmem((ranks, count, width), F32),
            vmem((count, 8, width), F32),
            vmem((8, half), F32),
            vmem((count + 1, 8, half), F32),
            vmem((taken, coarse), F32),
            vmem((2 * CHUNKS * taken, coarse // CHUNKS), BF16),
            vmem((count, half, half), BF16),
            vmem((taken, (count + 1) * half), F32),
            vmem((LANES, count * (half + width)), BF16),
            vmem((own_rows, LANES), F32),
            vmem((nz, 8, LANES), F32),
            vmem((nz // CHUNKS, ny * nx, 2, own_rows, LANES), F32),
            vmem((count, cases, width), F32),
            vmem((count, cases, width), F32),
            vmem((count, cases, half), F32),
            vmem((cases, half), F32),
            vmem((cases, half), F32),
            vmem((cases, half), F32),
            vmem((cases, half), F32),
            vmem((2 * nz, 8, LANES), F32),
            vmem((ny * nx, 8, LANES), F32),
            dma((7,)), dma((8,)), dma((8,)),
            dma((nz - 1,)), dma((nz - 1,)),
            dma((ny * nx - 1,)), dma((ny * nx - 1,)),
            dma((ny * nx,)), dma((ny * nx,)),
            dma((2 * nz - 1,)), dma((2 * nz - 1,)),
            dma((ny * nx - 1,)), dma((ny * nx - 1,)),
        ]
        projected, image, steps = pl.pallas_call(
            functools.partial(kernel, (nz, ny, nx)),
            out_shape=(field, field, jax.ShapeDtypeStruct((cases, LANES), F32)),
            in_specs=[pl.BlockSpec(memory_space=pltpu.HBM)] * 7,
            out_specs=(pl.BlockSpec(memory_space=pltpu.VMEM),) * 3,
            scratch_shapes=scratch,
            compiler_params=pltpu.CompilerParams(
                collective_id=0, has_side_effects=True, vmem_limit_bytes=48 << 20
            ),
        )(*(pltpu.with_memory_space_constraint(a, pltpu.HBM) for a in (residual, old_direction, matching, factor_inverse, rigid_modes.transpose(1, 0, 2), coarse_inverse, old_norms[None])))
        flat = lax.axis_index(both) * count + jnp.arange(count, dtype=jnp.int32)
        retain = (flat != count * lax.axis_size(both) - 1).astype(F32)[:, None, None]
        beta, alpha = steps[None, :, 0:1], steps[None, :, 1:2]
        direction = projected + beta * old_direction * retain
        return multipliers + alpha * direction, residual * retain - alpha * image, direction

    fields = P(both, None, None)
    return jax.shard_map(
        on_device,
        mesh=mesh,
        in_specs=(fields, fields, fields, P(), P(both, None), fields, fields, P(both, None)),
        out_specs=(fields, fields, fields),
        check_vma=False,
    )
```

```python
import functools

import jax
import jax.numpy as jnp
from jax import lax
from jax.experimental import pallas as pl
from jax.experimental.pallas import tpu as pltpu
from jax.sharding import PartitionSpec as P

F32 = jnp.float32
BF16 = jnp.bfloat16
HIGHEST = lax.Precision.HIGHEST
CHUNKS = 4
LANES = 128
NN = (((1,), (0,)), ((), ()))
NT = (((1,), (1,)), ((), ()))


def mm(a, b, dims=NN, precision=None):
    return lax.dot_general(a, b, dims, precision=precision, preferred_element_type=F32)


def pair(x):
    high = x.astype(BF16).astype(F32)
    return jnp.concatenate([high, x - high], 0).astype(BF16)


def joined(x):
    half = x.shape[0] // 2
    return x[:half] + x[half:]


def kernel(
    grid,
    res_h, old_h, mat_h, fac_h, rig_h, coa_h, onorm_h,
    p_out, w_out, ab_out,
    resf, oldf, onorm, mat, fac, rigt, rig, rhalo, nr, coa, relay, cpair, cpair2, table, ubig, lin, m24,
    zb, zb2, gat, gat2, inner_o, inner_m, w_o, face_o, face_p, ret_o, ret_p, arz, arp,
    local_sem, halo_send, halo_recv, z_send, z_recv, y_send, y_recv, c_send, c_recv,
    az_send, az_recv, ap_send, ap_recv, z2_send, z2_recv, y2_send, y2_recv, c2_send, c2_recv,
):
    nz, ny, nx = grid
    count, cases, half = p_out.shape
    width = 2 * half
    ranks = rig_h.shape[0]
    own_rows = count * ranks
    taken = coa.shape[0]
    span = coa.shape[1] // CHUNKS
    per_chunk = nz // CHUNKS
    s = lax.axis_index("sub")
    g = lax.axis_index("grp")
    z, y, x, core = s // ny, s % ny, g // 2, g % 2
    groups = 2 * nx
    flat = s * groups + g
    total = nz * ny * groups
    is_first = flat == 0
    is_last = flat == total - 1

    def of_flat(i):
        return (i // groups, i % groups)

    following = of_flat((flat + 1) % total)
    previous = of_flat((flat + total - 1) % total)
    partner = (s, x * 2 + 1 - core)
    second_next = of_flat((flat + 2) % total)
    second_previous = of_flat((flat + total - 2) % total)
    beyond = of_flat((flat + total + 2 - 4 * core) % total)
    def hops(i, ring):
        return min(i, ring - i)

    steps = sorted(range(1, nz), key=lambda i: -hops(i, nz))
    line = [(((z + i) % nz) * ny + y, g) for i in steps]
    across = [(((z + i) % nz) * ny + y, x * 2 + 1 - core) for i in steps]
    offsets = [(i, j) for i in range(ny) for j in range(nx) if i or j]
    offsets = sorted(offsets, key=lambda o: -hops(o[0], ny) - hops(o[1], nx))
    plane = [(z * ny + (y + i) % ny, ((x + j) % nx) * 2 + core) for i, j in offsets]
    slot = y * nx + x

    def to(src, dst, send, recv, device):
        return pltpu.make_async_remote_copy(
            src_ref=src, dst_ref=dst, send_sem=send, recv_sem=recv,
            device_id=device, device_id_type=pl.DeviceIdType.MESH,
        )

    def tell(semaphore, device):
        pl.semaphore_signal(
            semaphore, inc=1, device_id=device, device_id_type=pl.DeviceIdType.MESH
        )

    gat2[...] = jnp.zeros_like(gat2)
    barrier = pltpu.get_barrier_semaphore()
    everyone = [*plane, *line, *across, following, previous, partner, second_next, second_previous]
    for device in everyone:
        tell(barrier, device)
    loads = [
        pltpu.make_async_copy(mat_h, mat, local_sem.at[0]),
        pltpu.make_async_copy(rig_h, rigt, local_sem.at[1]),
        pltpu.make_async_copy(res_h, resf.at[pl.ds(1, count)], local_sem.at[2]),
        pltpu.make_async_copy(old_h, oldf.at[pl.ds(1, count)], local_sem.at[3]),
        pltpu.make_async_copy(coa_h, coa.at[pl.ds(8, own_rows)], local_sem.at[4]),
        pltpu.make_async_copy(fac_h, fac, local_sem.at[5]),
        pltpu.make_async_copy(onorm_h, onorm, local_sem.at[6]),
    ]
    for load in loads:
        load.start()
    ubig[...] = jnp.zeros_like(ubig)
    lin[...] = jnp.zeros_like(lin)
    rig[:, ranks:, :] = jnp.zeros((count, 8 - ranks, width), F32)

    loads[0].wait()
    unknowns = lax.broadcasted_iota(jnp.int32, (half, half), 0)
    for q in range(count):
        table[q] = jnp.where(unknowns == mat[pl.ds(q, 1), :], -1.0, 0.0).astype(BF16)
    loads[1].wait()
    for q in range(count):
        for m in range(ranks):
            rig[q, m : m + 1, :] = rigt[m, q : q + 1, :]
    for q in range(count):
        left = rig[q, :, :half]
        high = left.astype(BF16).astype(F32)
        mid = (left - high).astype(BF16).astype(F32)
        parts = jnp.concatenate([high, mid, left - high - mid], 0).astype(BF16)
        moved = mm(parts, table[q], NT)
        nr[q] = moved[:8] + moved[8:16] + moved[16:]

    rows = lax.broadcasted_iota(jnp.int32, (count * 8, LANES), 0)
    chunk = lax.broadcasted_iota(jnp.int32, (count * 8, LANES), 1) // cases
    loads[2].wait()
    resf[count] = jnp.where(is_last, 0.0, resf[count])
    rights = rig[:, :, half:].reshape(count * 8, half)
    lefts = nr[1:count].reshape((count - 1) * 8, half)
    own = resf[1:].reshape(count * cases, half)
    sums = mm(rights, own, NT, HIGHEST)
    before = mm(lefts, own, NT, HIGHEST)
    before = pltpu.roll(before, cases, 1)
    before = jnp.concatenate([jnp.zeros((8, LANES), F32), before], 0)
    sums = jnp.where(rows // 8 == chunk, sums + before, 0.0)
    sums = sums + pltpu.roll(sums, LANES // 2, 1)
    sums = sums + pltpu.roll(sums, LANES // 4, 1)
    for q in range(count):
        m24[q * ranks : (q + 1) * ranks, :] = sums[q * 8 : q * 8 + ranks]
    chunk = chunk[:8]
    tile = jnp.zeros((8, LANES), F32)
    for w in range(own_rows // 8):
        tile = jnp.where(chunk == w, m24[w * 8 : (w + 1) * 8, :], tile)
    faces = jnp.concatenate([pair(resf[count]), jnp.zeros((LANES - 2 * cases, half), BF16)], 0)
    zb[z] = tile
    pl.semaphore_wait(barrier, len(everyone))
    inside = pl.multiple_of((1 - core) * (own_rows - 8), 8)
    edge = pl.multiple_of(core * (own_rows + 8), 8)
    halo = [
        to(res_h.at[count - 1], resf.at[0], halo_send.at[0], halo_recv.at[0], following),
        to(nr.at[0], nr.at[count], halo_send.at[1], halo_recv.at[1], previous),
        to(rig.at[count - 1, :, pl.ds(half, half)], rhalo, halo_send.at[2], halo_recv.at[2], following),
        to(old_h.at[count - 1], oldf.at[0], halo_send.at[3], halo_recv.at[3], following),
        to(coa_h.at[pl.ds(inside, 8)], coa.at[pl.ds(edge, 8)], halo_send.at[4], halo_recv.at[4], partner),
        to(coa_h.at[pl.ds(own_rows - 8 - inside, 8)], relay, halo_send.at[5], halo_recv.at[5], partner),
    ]
    relayed = to(relay, coa.at[pl.ds(edge, 8)], halo_send.at[8], halo_recv.at[8], beyond)
    halo[1].start()

    def along_line(ref, at, send, recv, devices):
        copies = [to(ref.at[at], ref.at[at], send.at[i], recv.at[i], d) for i, d in enumerate(devices)]
        for copy in copies:
            copy.start()
        return copies

    def packed(ref, zl, w):
        block = jnp.zeros((8, LANES), F32)
        for a in range(CHUNKS):
            turned = ref[a * per_chunk + zl]
            if a != w:
                turned = pltpu.roll(turned, ((a - w) * cases) % LANES, 1)
            block = jnp.where(chunk == a, turned, block)
        return block

    def to_plane(ref, depth, send, recv, turn_send, turn_recv):
        def block(yx):
            return ref.at[:, yx, core, pl.ds(0, depth)]

        copies = [to(block(slot), block(slot), send.at[i], recv.at[i], d) for i, d in enumerate(plane)]
        for copy in copies:
            copy.start()
        turned = [to(block(slot), block(slot), turn_send.at[0], turn_recv.at[0], partner)]
        turned[0].start()

        def turn():
            for i in reversed(range(len(offsets))):
                dy, dx = offsets[i]
                copies[i].wait_recv()
                theirs = block(((y + ny - dy) % ny) * nx + (x + nx - dx) % nx)
                turned.append(to(theirs, theirs, turn_send.at[i + 1], turn_recv.at[i + 1], partner))
                turned[-1].start()

        return copies, turned, turn

    z_copies = along_line(zb, z, z_send, z_recv, line)
    for i in (5, 0, 3, 2, 4):
        halo[i].start()

    block = width // 4

    def forward(left, right, q):
        pairs = jnp.concatenate([mm(pair(left), table[q]).astype(BF16), pair(right)], 1)
        return jnp.concatenate(
            [
                joined(mm(pairs[:, : (i + 1) * block],
                          fac[q, i * block : (i + 1) * block, : (i + 1) * block], NT))
                for i in range(4)
            ], 1,
        )

    def backward(inner, q):
        pairs = pair(inner)
        solved = jnp.concatenate(
            [
                joined(mm(pairs[:, j * block :], fac[q, j * block :, j * block : (j + 1) * block]))
                for j in range(4)
            ], 1,
        )
        returned = joined(mm(pair(solved[:, :half]), table[q], NT))
        return solved[:, half:], returned

    def place(f, above):
        top = 2 + ranks * f + (0 if above else ranks)
        rows_of = (rhalo[:ranks] if f == 0 else rig[f - 1, :ranks, half:]) if above else nr[f, :ranks]
        if f in (0, count):
            rows_of = jnp.where(is_last if f else is_first, 0.0, rows_of)
        ubig[top : top + ranks, f * half : (f + 1) * half] = rows_of

    def keep(rows_of, values, columns):
        high = values.astype(BF16)
        low = (values - high.astype(F32)).astype(BF16)
        lin[rows_of[0] : rows_of[1], columns] = high
        lin[rows_of[0] + taken : rows_of[1] + taken, columns] = high
        lin[rows_of[0] + 2 * taken : rows_of[1] + 2 * taken, columns] = low

    def apply_all(q):
        low_row = (2 + ranks * q) // 8 * 8
        high_row = -(-(2 + ranks * (q + 3)) // 8) * 8
        sides = [
            jnp.concatenate(
                [oldf[f], resf[f], ubig[low_row:high_row, f * half : (f + 1) * half]], 0
            )
            for f in (q, q + 1)
        ]
        inner = forward(*sides, q)
        inner_o[q] = inner[:cases]
        inner_m[q] = inner[cases : 2 * cases]
        start = count * half + q * width
        keep((low_row, high_row), inner[2 * cases :], slice(start, start + width))

    for f in range(count + 1):
        if f > 0:
            place(f, True)
        if f < count:
            place(f, False)
    loads[3].wait()
    oldf[count] = jnp.where(is_last, 0.0, oldf[count])
    loads[5].wait()
    apply_all(1)
    halo[5].wait_recv()
    relayed.start()
    for q in range(2, count - 1):
        apply_all(q)
    halo[1].wait_recv()
    added = mm(pair(nr[count]), faces, NT)
    added = added[:8] + pltpu.roll(added[:8], LANES - cases, 1) + added[8:]
    zb2[z] = jnp.where(chunk == 0, added, 0.0)
    z2_copies = along_line(zb2, z, z2_send, z2_recv, line)

    for copy in reversed(z_copies):
        copy.wait()
    for zl in range(per_chunk):
        for w in range(own_rows // 8):
            gat[zl, slot, core, w * 8 : (w + 1) * 8, :] = packed(zb, zl, w)
    y_copies, c_copies, turn = to_plane(gat, own_rows, y_send, y_recv, c_send, c_recv)
    def take_back(q):
        solved, returned = backward(inner_o[q], q)
        w_o[q] = solved if q else solved + w_o[0]
        if q == 1:
            w_o[0] = returned
        elif q:
            w_o[q - 1] += returned
        else:
            ret_o[...] = returned

    for q in range(1, count - 1):
        take_back(q)
    for copy in reversed(z2_copies):
        copy.wait()
    for zl in range(per_chunk):
        gat2[zl, slot, core, :ranks] = packed(zb2, zl, 0)[:ranks]
    y2_copies, c2_copies, turn2 = to_plane(gat2, ranks, y2_send, y2_recv, c2_send, c2_recv)
    halo[0].wait_recv()
    halo[2].wait_recv()
    halo[3].wait_recv()
    resf[0] = jnp.where(is_first, 0.0, resf[0])
    place(0, True)
    place(count, False)
    oldf[0] = jnp.where(is_first, 0.0, oldf[0])
    for q in (0, count - 1):
        apply_all(q)
    keep((0, taken), ubig[:, half:], slice(0, count * half))
    take_back(0)
    ret_o_copy = to(ret_o, face_o, halo_send.at[6], halo_recv.at[6], previous)
    ret_o_copy.start()
    take_back(count - 1)
    loads[4].wait()
    halo[4].wait_recv()
    relayed.wait_recv()
    period = min(LANES // 8 * own_rows, span)
    kept = period // own_rows * 8
    source = lax.broadcasted_iota(jnp.int32, (period, kept), 0)
    target = lax.broadcasted_iota(jnp.int32, (period, kept), 1)
    chosen = jnp.where(source == target // 8 * own_rows + target % 8, 1.0, 0.0).astype(BF16)
    following_rows = pltpu.roll(coa[...], coa.shape[1] - own_rows, 1)
    for a in range(CHUNKS):
        part = slice(a * span, (a + 1) * span)
        rows_of = slice(a * 2 * taken, (a + 1) * 2 * taken)
        cpair[rows_of] = pair(coa[:, part])
        shifted = pair(following_rows[:, part])
        cpair2[rows_of] = jnp.concatenate(
            [mm(shifted[:, k : k + period], chosen) for k in range(0, span, period)], 1
        ).astype(BF16)

    turn()
    turn2()
    for copy in c_copies:
        copy.wait_recv()

    def product(rows_of, gathered):
        high = gathered.astype(BF16)
        low = (gathered - high.astype(F32)).astype(BF16)
        both = mm(rows_of[...], jnp.concatenate([high, low], 1))
        return both[:, :LANES] + both[:, LANES:]

    products = product(cpair, gat[...].reshape(span, LANES))
    for copy in c2_copies:
        copy.wait_recv()
    products = products + product(cpair2, gat2[...].reshape(span // own_rows * 8, LANES))
    chunk_all = lax.broadcasted_iota(jnp.int32, (taken, LANES), 1) // cases
    coeffs = jnp.zeros((taken, LANES), F32)
    for a in range(CHUNKS):
        coeffs = jnp.where(chunk_all == a, joined(products[a * 2 * taken : (a + 1) * 2 * taken]), coeffs)
    coeffs = coeffs + pltpu.roll(coeffs, LANES // 2, 1)
    coeffs = coeffs + pltpu.roll(coeffs, LANES // 4, 1)
    high = coeffs.astype(BF16).astype(F32)
    thrice = jnp.concatenate(
        [high, coeffs - high, high, jnp.zeros((LANES - 3 * taken, LANES), F32)], 0
    ).T[:cases].astype(BF16)
    moved = mm(thrice, lin[...])
    norms, pp, po, oo = (jnp.zeros((cases, 1), F32) for _ in range(4))
    inners = []
    for q in range(count):
        part = resf[q + 1] - moved[:, q * half : (q + 1) * half]
        p_out[q] = part
        start = count * half + q * width
        inner = inner_m[q] - moved[:, start : start + width]
        inners.append(inner)
        old_inner = inner_o[q]
        norms = norms + jnp.sum(part * part, 1, keepdims=True)
        pp = pp + jnp.sum(inner * inner, 1, keepdims=True)
        po = po + jnp.sum(inner * old_inner, 1, keepdims=True)
        oo = oo + jnp.sum(old_inner * old_inner, 1, keepdims=True)

    lane = lax.broadcasted_iota(jnp.int32, (cases, LANES), 1)
    square = jnp.zeros((cases, LANES), F32)
    for i, column in enumerate((norms, pp, po, oo)):
        square = jnp.where(lane == i, column, square)
    square = jnp.concatenate([square, jnp.zeros((LANES - cases, LANES), F32)], 0).T
    here = 2 * z + core
    arz[here] = square[0:1] + sum(pltpu.roll(square[i : i + 1], i * cases, 1) for i in range(1, CHUNKS))
    pairs_of = [device for both in zip(line, across) for device in both]
    az_copies = along_line(arz, here, az_send, az_recv, [*pairs_of, partner])

    for q in range(count):
        solved, returned = backward(inners[q], q)
        w_out[q] = solved
        if q:
            w_out[q - 1] += returned
        else:
            ret_p[...] = returned
            ret_p_copy = to(ret_p, face_p, halo_send.at[7], halo_recv.at[7], previous)
            ret_p_copy.start()
    for copy in reversed(az_copies):
        copy.wait()
    arp[slot] = sum(arz[i] for i in range(2 * nz))
    ap_copies = along_line(arp, slot, ap_send, ap_recv, plane)
    loads[6].wait()
    ret_o_copy.wait()
    ret_p_copy.wait()
    w_o[count - 1] = jnp.where(is_last, 0.0, w_o[count - 1] + face_o[...])
    w_out[count - 1] = jnp.where(is_last, 0.0, w_out[count - 1] + face_p[...])
    for copy in (*halo, relayed, *y_copies, *c_copies, *y2_copies, *c2_copies):
        copy.wait_send()
    for copy in reversed(ap_copies):
        copy.wait()
    totals = sum(arp[i] for i in range(ny * nx))
    norm, pure, mixed, old_part = (pltpu.roll(totals, (-i * cases) % LANES, 1) if i else totals for i in range(CHUNKS))
    beta = norm / jnp.concatenate([onorm[...], jnp.ones((1, LANES - cases), F32)], 1)
    curvature = pure + 2.0 * beta * mixed + beta * beta * old_part
    alpha = norm / curvature
    row = lax.broadcasted_iota(jnp.int32, (LANES, LANES), 0)
    square = jnp.where(row == 0, beta, jnp.where(row == 1, alpha, 0.0)).T
    ab_out[0] = jnp.broadcast_to(square[:cases, 0:1], (cases, half))
    ab_out[1] = jnp.broadcast_to(square[:cases, 1:2], (cases, half))
    column = square[:cases, 0:1]
    for q in range(count):
        w_out[q] += column * w_o[q]


def solution(mesh, ny=4):
    nz, nx = mesh.shape["sub"] // ny, mesh.shape["grp"] // 2
    both = ("sub", "grp")

    def on_device(multipliers, residual, old_direction, old_norms, matching, factor_inverse, rigid_modes, coarse_inverse):
        count, cases, half = multipliers.shape
        ranks = rigid_modes.shape[1]
        own_rows = count * ranks
        width = 2 * half
        coarse = coarse_inverse.shape[1]
        field = jax.ShapeDtypeStruct((count, cases, half), F32)
        dma = pltpu.SemaphoreType.DMA
        taken = own_rows + 16
        vmem = pltpu.VMEM
        scratch = [
            vmem((count + 1, cases, half), F32),
            vmem((count + 1, cases, half), F32),
            vmem((1, cases), F32),
            vmem((count, half), jnp.int32),
            vmem((count, width, width), BF16),
            vmem((ranks, count, width), F32),
            vmem((count, 8, width), F32),
            vmem((8, half), F32),
            vmem((count + 1, 8, half), F32),
            vmem((taken, coarse), F32),
            vmem((8, coarse), F32),
            vmem((2 * CHUNKS * taken, coarse // CHUNKS), BF16),
            vmem((2 * CHUNKS * taken, coarse // CHUNKS // own_rows * 8), BF16),
            vmem((count, half, half), BF16),
            vmem((taken, (count + 1) * half), F32),
            vmem((LANES, count * (half + width)), BF16),
            vmem((own_rows, LANES), F32),
            vmem((nz, 8, LANES), F32),
            vmem((nz, 8, LANES), F32),
            vmem((nz // CHUNKS, ny * nx, 2, own_rows, LANES), F32),
            vmem((nz // CHUNKS, ny * nx, 2, 8, LANES), F32),
            vmem((count, cases, width), F32),
            vmem((count, cases, width), F32),
            vmem((count, cases, half), F32),
            vmem((cases, half), F32),
            vmem((cases, half), F32),
            vmem((cases, half), F32),
            vmem((cases, half), F32),
            vmem((2 * nz, 1, LANES), F32),
            vmem((ny * nx, 1, LANES), F32),
            dma((7,)), dma((9,)), dma((9,)),
            dma((nz - 1,)), dma((nz - 1,)),
            dma((ny * nx - 1,)), dma((ny * nx - 1,)),
            dma((ny * nx,)), dma((ny * nx,)),
            dma((2 * nz - 1,)), dma((2 * nz - 1,)),
            dma((ny * nx - 1,)), dma((ny * nx - 1,)),
            dma((nz - 1,)), dma((nz - 1,)),
            dma((ny * nx - 1,)), dma((ny * nx - 1,)),
            dma((ny * nx,)), dma((ny * nx,)),
        ]
        projected, image, steps = pl.pallas_call(
            functools.partial(kernel, (nz, ny, nx)),
            out_shape=(field, field, jax.ShapeDtypeStruct((2, cases, half), F32)),
            in_specs=[pl.BlockSpec(memory_space=pltpu.HBM)] * 7,
            out_specs=(pl.BlockSpec(memory_space=pltpu.VMEM),) * 3,
            scratch_shapes=scratch,
            compiler_params=pltpu.CompilerParams(
                collective_id=0, has_side_effects=True, vmem_limit_bytes=48 << 20
            ),
        )(*(pltpu.with_memory_space_constraint(a, pltpu.HBM) for a in (residual, old_direction, matching, factor_inverse, rigid_modes.transpose(1, 0, 2), coarse_inverse, old_norms[None])))
        flat = lax.axis_index(both) * count + jnp.arange(count, dtype=jnp.int32)
        retain = (flat != count * lax.axis_size(both) - 1).astype(F32)[:, None, None]
        beta, alpha = steps[0:1], steps[1:2]
        direction = projected + beta * old_direction * retain
        return multipliers + alpha * direction, residual * retain - alpha * image, direction

    fields = P(both, None, None)
    return jax.shard_map(
        on_device,
        mesh=mesh,
        in_specs=(fields, fields, fields, P(), P(both, None), fields, fields, P(both, None)),
        out_specs=(fields, fields, fields),
        check_vma=False,
    )
```

```python
import functools

import jax
import jax.numpy as jnp
from jax import lax
from jax.experimental import pallas as pl
from jax.experimental.pallas import tpu as pltpu
from jax.sharding import PartitionSpec as P

F32 = jnp.float32
BF16 = jnp.bfloat16
HIGHEST = lax.Precision.HIGHEST
CHUNKS = 4
LANES = 128
NN = (((1,), (0,)), ((), ()))
NT = (((1,), (1,)), ((), ()))


def mm(a, b, dims=NN, precision=None):
    return lax.dot_general(a, b, dims, precision=precision, preferred_element_type=F32)


def pair(x):
    high = x.astype(BF16).astype(F32)
    return jnp.concatenate([high, x - high], 0).astype(BF16)


def joined(x):
    half = x.shape[0] // 2
    return x[:half] + x[half:]


def kernel(
    grid,
    res_h, old_h, mat_h, fac_h, rig_h, coa_h, onorm_h,
    p_out, w_out, ab_out,
    resf, oldf, onorm, mat, fac, rigt, rig, rhalo, nr, coa, relay, cpair, cpair2, table, ubig, lin, m24,
    zb, zb2, gat, gat2, inner_o, inner_m, w_o, face_o, face_p, ret_o, ret_p, arz, arp,
    local_sem, halo_send, halo_recv, z_send, z_recv, y_send, y_recv, c_send, c_recv,
    az_send, az_recv, ap_send, ap_recv, z2_send, z2_recv, y2_send, y2_recv, c2_send, c2_recv,
):
    nz, ny, nx = grid
    count, cases, half = p_out.shape
    width = 2 * half
    ranks = rig_h.shape[0]
    own_rows = count * ranks
    taken = coa.shape[0]
    span = coa.shape[1] // CHUNKS
    per_chunk = nz // CHUNKS
    s = lax.axis_index("sub")
    g = lax.axis_index("grp")
    z, y, x, core = s // ny, s % ny, g // 2, g % 2
    groups = 2 * nx
    flat = s * groups + g
    total = nz * ny * groups
    is_first = flat == 0
    is_last = flat == total - 1

    def of_flat(i):
        return (i // groups, i % groups)

    following = of_flat((flat + 1) % total)
    previous = of_flat((flat + total - 1) % total)
    partner = (s, x * 2 + 1 - core)
    second_next = of_flat((flat + 2) % total)
    second_previous = of_flat((flat + total - 2) % total)
    beyond = of_flat((flat + total + 2 - 4 * core) % total)
    def hops(i, ring):
        return min(i, ring - i)

    steps = sorted(range(1, nz), key=lambda i: -hops(i, nz))
    line = [(((z + i) % nz) * ny + y, g) for i in steps]
    across = [(((z + i) % nz) * ny + y, x * 2 + 1 - core) for i in steps]
    offsets = [(i, j) for i in range(ny) for j in range(nx) if i or j]
    offsets = sorted(offsets, key=lambda o: -hops(o[0], ny) - hops(o[1], nx))
    plane = [(z * ny + (y + i) % ny, ((x + j) % nx) * 2 + core) for i, j in offsets]
    slot = y * nx + x

    def to(src, dst, send, recv, device):
        return pltpu.make_async_remote_copy(
            src_ref=src, dst_ref=dst, send_sem=send, recv_sem=recv,
            device_id=device, device_id_type=pl.DeviceIdType.MESH,
        )

    def tell(semaphore, device):
        pl.semaphore_signal(
            semaphore, inc=1, device_id=device, device_id_type=pl.DeviceIdType.MESH
        )

    gat2[...] = jnp.zeros_like(gat2)
    barrier = pltpu.get_barrier_semaphore()
    everyone = [*plane, *line, *across, following, previous, partner, second_next, second_previous]
    for device in everyone:
        tell(barrier, device)
    loads = [
        pltpu.make_async_copy(mat_h, mat, local_sem.at[0]),
        pltpu.make_async_copy(rig_h, rigt, local_sem.at[1]),
        pltpu.make_async_copy(res_h, resf.at[pl.ds(1, count)], local_sem.at[2]),
        pltpu.make_async_copy(old_h, oldf.at[pl.ds(1, count)], local_sem.at[3]),
        pltpu.make_async_copy(coa_h, coa.at[pl.ds(8, own_rows)], local_sem.at[4]),
        pltpu.make_async_copy(fac_h, fac, local_sem.at[5]),
        pltpu.make_async_copy(onorm_h, onorm, local_sem.at[6]),
    ]
    for load in loads:
        load.start()
    ubig[...] = jnp.zeros_like(ubig)
    lin[...] = jnp.zeros_like(lin)
    rig[:, ranks:, :] = jnp.zeros((count, 8 - ranks, width), F32)

    loads[0].wait()
    unknowns = lax.broadcasted_iota(jnp.int32, (half, half), 0)
    for q in range(count):
        table[q] = jnp.where(unknowns == mat[pl.ds(q, 1), :], -1.0, 0.0).astype(BF16)
    loads[1].wait()
    for q in range(count):
        for m in range(ranks):
            rig[q, m : m + 1, :] = rigt[m, q : q + 1, :]
    for q in range(count):
        left = rig[q, :, :half]
        high = left.astype(BF16).astype(F32)
        mid = (left - high).astype(BF16).astype(F32)
        parts = jnp.concatenate([high, mid, left - high - mid], 0).astype(BF16)
        moved = mm(parts, table[q], NT)
        nr[q] = moved[:8] + moved[8:16] + moved[16:]

    rows = lax.broadcasted_iota(jnp.int32, (count * 8, LANES), 0)
    chunk = lax.broadcasted_iota(jnp.int32, (count * 8, LANES), 1) // cases
    loads[2].wait()
    resf[count] = jnp.where(is_last, 0.0, resf[count])
    rights = rig[:, :, half:].reshape(count * 8, half)
    lefts = nr[1:count].reshape((count - 1) * 8, half)
    own = resf[1:].reshape(count * cases, half)
    sums = mm(rights, own, NT, HIGHEST)
    before = mm(lefts, own, NT, HIGHEST)
    before = pltpu.roll(before, cases, 1)
    before = jnp.concatenate([jnp.zeros((8, LANES), F32), before], 0)
    sums = jnp.where(rows // 8 == chunk, sums + before, 0.0)
    sums = sums + pltpu.roll(sums, LANES // 2, 1)
    sums = sums + pltpu.roll(sums, LANES // 4, 1)
    for q in range(count):
        m24[q * ranks : (q + 1) * ranks, :] = sums[q * 8 : q * 8 + ranks]
    chunk = chunk[:8]
    tile = jnp.zeros((8, LANES), F32)
    for w in range(own_rows // 8):
        tile = jnp.where(chunk == w, m24[w * 8 : (w + 1) * 8, :], tile)
    faces = jnp.concatenate([pair(resf[count]), jnp.zeros((LANES - 2 * cases, half), BF16)], 0)
    zb[z] = tile
    pl.semaphore_wait(barrier, len(everyone))
    inside = pl.multiple_of((1 - core) * (own_rows - 8), 8)
    edge = pl.multiple_of(core * (own_rows + 8), 8)
    halo = [
        to(res_h.at[count - 1], resf.at[0], halo_send.at[0], halo_recv.at[0], following),
        to(nr.at[0], nr.at[count], halo_send.at[1], halo_recv.at[1], previous),
        to(rig.at[count - 1, :, pl.ds(half, half)], rhalo, halo_send.at[2], halo_recv.at[2], following),
        to(old_h.at[count - 1], oldf.at[0], halo_send.at[3], halo_recv.at[3], following),
        to(coa_h.at[pl.ds(inside, 8)], coa.at[pl.ds(edge, 8)], halo_send.at[4], halo_recv.at[4], partner),
        to(coa_h.at[pl.ds(own_rows - 8 - inside, 8)], relay, halo_send.at[5], halo_recv.at[5], partner),
    ]
    relayed = to(relay, coa.at[pl.ds(edge, 8)], halo_send.at[8], halo_recv.at[8], beyond)

    @pl.when(jnp.logical_not(is_first))
    def _():
        halo[1].start()


    def along_line(ref, at, send, recv, devices):
        copies = [to(ref.at[at], ref.at[at], send.at[i], recv.at[i], d) for i, d in enumerate(devices)]
        for copy in copies:
            copy.start()
        return copies

    def packed(ref, zl, w):
        block = jnp.zeros((8, LANES), F32)
        for a in range(CHUNKS):
            turned = ref[a * per_chunk + zl]
            if a != w:
                turned = pltpu.roll(turned, ((a - w) * cases) % LANES, 1)
            block = jnp.where(chunk == a, turned, block)
        return block

    def to_plane(ref, depth, send, recv, turn_send, turn_recv):
        def block(yx):
            return ref.at[:, yx, core, pl.ds(0, depth)]

        copies = [to(block(slot), block(slot), send.at[i], recv.at[i], d) for i, d in enumerate(plane)]
        for copy in copies:
            copy.start()
        turned = [to(block(slot), block(slot), turn_send.at[0], turn_recv.at[0], partner)]
        turned[0].start()

        def turn():
            for i in reversed(range(len(offsets))):
                dy, dx = offsets[i]
                copies[i].wait_recv()
                theirs = block(((y + ny - dy) % ny) * nx + (x + nx - dx) % nx)
                turned.append(to(theirs, theirs, turn_send.at[i + 1], turn_recv.at[i + 1], partner))
                turned[-1].start()

        return copies, turned, turn

    z_copies = along_line(zb, z, z_send, z_recv, line)
    for i in (5, 0, 3, 2, 4):
        halo[i].start()

    block = width // 4

    def forward(left, right, q):
        pairs = jnp.concatenate([mm(pair(left), table[q]).astype(BF16), pair(right)], 1)
        return jnp.concatenate(
            [
                joined(mm(pairs[:, : (i + 1) * block],
                          fac[q, i * block : (i + 1) * block, : (i + 1) * block], NT))
                for i in range(4)
            ], 1,
        )

    def backward(inner, q):
        pairs = pair(inner)
        solved = jnp.concatenate(
            [
                joined(mm(pairs[:, j * block :], fac[q, j * block :, j * block : (j + 1) * block]))
                for j in range(4)
            ], 1,
        )
        returned = joined(mm(pair(solved[:, :half]), table[q], NT))
        return solved[:, half:], returned

    def place(f, above):
        top = 2 + ranks * f + (0 if above else ranks)
        rows_of = (rhalo[:ranks] if f == 0 else rig[f - 1, :ranks, half:]) if above else nr[f, :ranks]
        if f in (0, count):
            rows_of = jnp.where(is_last if f else is_first, 0.0, rows_of)
        ubig[top : top + ranks, f * half : (f + 1) * half] = rows_of

    def keep(rows_of, values, columns):
        high = values.astype(BF16)
        low = (values - high.astype(F32)).astype(BF16)
        lin[rows_of[0] : rows_of[1], columns] = high
        lin[rows_of[0] + taken : rows_of[1] + taken, columns] = high
        lin[rows_of[0] + 2 * taken : rows_of[1] + 2 * taken, columns] = low

    def apply_all(q):
        low_row = (2 + ranks * q) // 8 * 8
        high_row = -(-(2 + ranks * (q + 3)) // 8) * 8
        sides = [
            jnp.concatenate(
                [oldf[f], resf[f], ubig[low_row:high_row, f * half : (f + 1) * half]], 0
            )
            for f in (q, q + 1)
        ]
        inner = forward(*sides, q)
        inner_o[q] = inner[:cases]
        inner_m[q] = inner[cases : 2 * cases]
        start = count * half + q * width
        keep((low_row, high_row), inner[2 * cases :], slice(start, start + width))

    for f in range(count + 1):
        if f > 0:
            place(f, True)
        if f < count:
            place(f, False)
    loads[3].wait()
    oldf[count] = jnp.where(is_last, 0.0, oldf[count])
    loads[5].wait()
    apply_all(1)
    halo[5].wait_recv()
    relayed.start()
    for q in range(2, count - 1):
        apply_all(q)
    z2_copies = [to(zb2.at[z], zb2.at[z], z2_send.at[i], z2_recv.at[i], d) for i, d in enumerate(line)]

    def send_corrections():
        @pl.when(jnp.logical_not(is_last))
        def _():
            halo[1].wait_recv()

        added = mm(pair(jnp.where(is_last, 0.0, nr[count])), faces, NT)
        added = added[:8] + pltpu.roll(added[:8], LANES - cases, 1) + added[8:]
        zb2[z] = jnp.where(chunk == 0, added, 0.0)
        for copy in z2_copies:
            copy.start()

    far_next = jnp.logical_and(jnp.logical_and(x == nx - 1, y == ny - 1), core == 1)
    pl.when(jnp.logical_not(far_next))(send_corrections)
    for copy in reversed(z_copies):
        copy.wait()
    for zl in range(per_chunk):
        for w in range(own_rows // 8):
            gat[zl, slot, core, w * 8 : (w + 1) * 8, :] = packed(zb, zl, w)
    y_copies, c_copies, turn = to_plane(gat, own_rows, y_send, y_recv, c_send, c_recv)
    pl.when(far_next)(send_corrections)
    def take_back(q):
        solved, returned = backward(inner_o[q], q)
        w_o[q] = solved if q else solved + w_o[0]
        if q == 1:
            w_o[0] = returned
        elif q:
            w_o[q - 1] += returned
        else:
            ret_o[...] = returned

    for q in range(1, count - 1):
        take_back(q)
    for copy in reversed(z2_copies):
        copy.wait()
    for zl in range(per_chunk):
        gat2[zl, slot, core, :ranks] = packed(zb2, zl, 0)[:ranks]
    y2_copies, c2_copies, turn2 = to_plane(gat2, ranks, y2_send, y2_recv, c2_send, c2_recv)
    halo[0].wait_recv()
    halo[2].wait_recv()
    halo[3].wait_recv()
    resf[0] = jnp.where(is_first, 0.0, resf[0])
    place(0, True)
    place(count, False)
    oldf[0] = jnp.where(is_first, 0.0, oldf[0])
    for q in (0, count - 1):
        apply_all(q)
    keep((0, taken), ubig[:, half:], slice(0, count * half))
    take_back(0)
    ret_o_copy = to(ret_o, face_o, halo_send.at[6], halo_recv.at[6], previous)
    ret_o_copy.start()
    take_back(count - 1)
    loads[4].wait()
    halo[4].wait_recv()
    relayed.wait_recv()
    period = min(LANES // 8 * own_rows, span)
    kept = period // own_rows * 8
    source = lax.broadcasted_iota(jnp.int32, (period, kept), 0)
    target = lax.broadcasted_iota(jnp.int32, (period, kept), 1)
    chosen = jnp.where(source == target // 8 * own_rows + target % 8, 1.0, 0.0).astype(BF16)
    following_rows = pltpu.roll(coa[...], coa.shape[1] - own_rows, 1)
    for a in range(CHUNKS):
        part = slice(a * span, (a + 1) * span)
        rows_of = slice(a * 2 * taken, (a + 1) * 2 * taken)
        cpair[rows_of] = pair(coa[:, part])
        shifted = pair(following_rows[:, part])
        cpair2[rows_of] = jnp.concatenate(
            [mm(shifted[:, k : k + period], chosen) for k in range(0, span, period)], 1
        ).astype(BF16)

    turn()
    turn2()
    for copy in c_copies:
        copy.wait_recv()

    def product(rows_of, gathered):
        high = gathered.astype(BF16)
        low = (gathered - high.astype(F32)).astype(BF16)
        both = mm(rows_of[...], jnp.concatenate([high, low], 1))
        return both[:, :LANES] + both[:, LANES:]

    products = product(cpair, gat[...].reshape(span, LANES))
    for copy in c2_copies:
        copy.wait_recv()
    products = products + product(cpair2, gat2[...].reshape(span // own_rows * 8, LANES))
    chunk_all = lax.broadcasted_iota(jnp.int32, (taken, LANES), 1) // cases
    coeffs = jnp.zeros((taken, LANES), F32)
    for a in range(CHUNKS):
        coeffs = jnp.where(chunk_all == a, joined(products[a * 2 * taken : (a + 1) * 2 * taken]), coeffs)
    coeffs = coeffs + pltpu.roll(coeffs, LANES // 2, 1)
    coeffs = coeffs + pltpu.roll(coeffs, LANES // 4, 1)
    high = coeffs.astype(BF16).astype(F32)
    thrice = jnp.concatenate(
        [high, coeffs - high, high, jnp.zeros((LANES - 3 * taken, LANES), F32)], 0
    ).T[:cases].astype(BF16)
    moved = mm(thrice, lin[...])
    norms, pp, po, oo = (jnp.zeros((cases, 1), F32) for _ in range(4))
    inners = []
    for q in range(count):
        part = resf[q + 1] - moved[:, q * half : (q + 1) * half]
        p_out[q] = part
        start = count * half + q * width
        inner = inner_m[q] - moved[:, start : start + width]
        inners.append(inner)
        old_inner = inner_o[q]
        norms = norms + jnp.sum(part * part, 1, keepdims=True)
        pp = pp + jnp.sum(inner * inner, 1, keepdims=True)
        po = po + jnp.sum(inner * old_inner, 1, keepdims=True)
        oo = oo + jnp.sum(old_inner * old_inner, 1, keepdims=True)

    lane = lax.broadcasted_iota(jnp.int32, (cases, LANES), 1)
    square = jnp.zeros((cases, LANES), F32)
    for i, column in enumerate((norms, pp, po, oo)):
        square = jnp.where(lane == i, column, square)
    square = jnp.concatenate([square, jnp.zeros((LANES - cases, LANES), F32)], 0).T
    here = 2 * z + core
    arz[here] = square[0:1] + sum(pltpu.roll(square[i : i + 1], i * cases, 1) for i in range(1, CHUNKS))
    pairs_of = [device for both in zip(line, across) for device in both]
    az_copies = along_line(arz, here, az_send, az_recv, [*pairs_of, partner])

    for q in range(count):
        solved, returned = backward(inners[q], q)
        w_out[q] = solved
        if q:
            w_out[q - 1] += returned
        else:
            ret_p[...] = returned
            ret_p_copy = to(ret_p, face_p, halo_send.at[7], halo_recv.at[7], previous)
            ret_p_copy.start()
    for copy in reversed(az_copies):
        copy.wait()
    arp[slot] = sum(arz[i] for i in range(2 * nz))
    ap_copies = along_line(arp, slot, ap_send, ap_recv, plane)
    loads[6].wait()
    ret_o_copy.wait()
    ret_p_copy.wait()
    w_o[count - 1] = jnp.where(is_last, 0.0, w_o[count - 1] + face_o[...])
    w_out[count - 1] = jnp.where(is_last, 0.0, w_out[count - 1] + face_p[...])
    @pl.when(jnp.logical_not(is_first))
    def _():
        halo[1].wait_send()

    for copy in (halo[0], *halo[2:], relayed, *y_copies, *c_copies, *y2_copies, *c2_copies):
        copy.wait_send()
    for copy in reversed(ap_copies):
        copy.wait()
    totals = sum(arp[i] for i in range(ny * nx))
    norm, pure, mixed, old_part = (pltpu.roll(totals, (-i * cases) % LANES, 1) if i else totals for i in range(CHUNKS))
    beta = norm / jnp.concatenate([onorm[...], jnp.ones((1, LANES - cases), F32)], 1)
    curvature = pure + 2.0 * beta * mixed + beta * beta * old_part
    alpha = norm / curvature
    row = lax.broadcasted_iota(jnp.int32, (LANES, LANES), 0)
    square = jnp.where(row == 0, beta, jnp.where(row == 1, alpha, 0.0)).T
    ab_out[0] = jnp.broadcast_to(square[:cases, 0:1], (cases, half))
    ab_out[1] = jnp.broadcast_to(square[:cases, 1:2], (cases, half))
    column = square[:cases, 0:1]
    for q in range(count):
        w_out[q] += column * w_o[q]


def solution(mesh, ny=4):
    nz, nx = mesh.shape["sub"] // ny, mesh.shape["grp"] // 2
    both = ("sub", "grp")

    def on_device(multipliers, residual, old_direction, old_norms, matching, factor_inverse, rigid_modes, coarse_inverse):
        count, cases, half = multipliers.shape
        ranks = rigid_modes.shape[1]
        own_rows = count * ranks
        width = 2 * half
        coarse = coarse_inverse.shape[1]
        field = jax.ShapeDtypeStruct((count, cases, half), F32)
        dma = pltpu.SemaphoreType.DMA
        taken = own_rows + 16
        vmem = pltpu.VMEM
        scratch = [
            vmem((count + 1, cases, half), F32),
            vmem((count + 1, cases, half), F32),
            vmem((1, cases), F32),
            vmem((count, half), jnp.int32),
            vmem((count, width, width), BF16),
            vmem((ranks, count, width), F32),
            vmem((count, 8, width), F32),
            vmem((8, half), F32),
            vmem((count + 1, 8, half), F32),
            vmem((taken, coarse), F32),
            vmem((8, coarse), F32),
            vmem((2 * CHUNKS * taken, coarse // CHUNKS), BF16),
            vmem((2 * CHUNKS * taken, coarse // CHUNKS // own_rows * 8), BF16),
            vmem((count, half, half), BF16),
            vmem((taken, (count + 1) * half), F32),
            vmem((LANES, count * (half + width)), BF16),
            vmem((own_rows, LANES), F32),
            vmem((nz, 8, LANES), F32),
            vmem((nz, 8, LANES), F32),
            vmem((nz // CHUNKS, ny * nx, 2, own_rows, LANES), F32),
            vmem((nz // CHUNKS, ny * nx, 2, 8, LANES), F32),
            vmem((count, cases, width), F32),
            vmem((count, cases, width), F32),
            vmem((count, cases, half), F32),
            vmem((cases, half), F32),
            vmem((cases, half), F32),
            vmem((cases, half), F32),
            vmem((cases, half), F32),
            vmem((2 * nz, 1, LANES), F32),
            vmem((ny * nx, 1, LANES), F32),
            dma((7,)), dma((9,)), dma((9,)),
            dma((nz - 1,)), dma((nz - 1,)),
            dma((ny * nx - 1,)), dma((ny * nx - 1,)),
            dma((ny * nx,)), dma((ny * nx,)),
            dma((2 * nz - 1,)), dma((2 * nz - 1,)),
            dma((ny * nx - 1,)), dma((ny * nx - 1,)),
            dma((nz - 1,)), dma((nz - 1,)),
            dma((ny * nx - 1,)), dma((ny * nx - 1,)),
            dma((ny * nx,)), dma((ny * nx,)),
        ]
        projected, image, steps = pl.pallas_call(
            functools.partial(kernel, (nz, ny, nx)),
            out_shape=(field, field, jax.ShapeDtypeStruct((2, cases, half), F32)),
            in_specs=[pl.BlockSpec(memory_space=pltpu.HBM)] * 7,
            out_specs=(pl.BlockSpec(memory_space=pltpu.VMEM),) * 3,
            scratch_shapes=scratch,
            compiler_params=pltpu.CompilerParams(
                collective_id=0, has_side_effects=True, vmem_limit_bytes=48 << 20
            ),
        )(*(pltpu.with_memory_space_constraint(a, pltpu.HBM) for a in (residual, old_direction, matching, factor_inverse, rigid_modes.transpose(1, 0, 2), coarse_inverse, old_norms[None])))
        flat = lax.axis_index(both) * count + jnp.arange(count, dtype=jnp.int32)
        retain = (flat != count * lax.axis_size(both) - 1).astype(F32)[:, None, None]
        beta, alpha = steps[0:1], steps[1:2]
        direction = projected + beta * old_direction * retain
        return multipliers + alpha * direction, residual * retain - alpha * image, direction

    fields = P(both, None, None)
    return jax.shard_map(
        on_device,
        mesh=mesh,
        in_specs=(fields, fields, fields, P(), P(both, None), fields, fields, P(both, None)),
        out_specs=(fields, fields, fields),
        check_vma=False,
    )
```

```python
import functools

import jax
import jax.numpy as jnp
from jax import lax
from jax.experimental import pallas as pl
from jax.experimental.pallas import tpu as pltpu
from jax.sharding import PartitionSpec as P

F32 = jnp.float32
BF16 = jnp.bfloat16
HIGHEST = lax.Precision.HIGHEST
CHUNKS = 4
LANES = 128
NN = (((1,), (0,)), ((), ()))
NT = (((1,), (1,)), ((), ()))


def mm(a, b, dims=NN, precision=None):
    return lax.dot_general(a, b, dims, precision=precision, preferred_element_type=F32)


def pair(x):
    high = x.astype(BF16).astype(F32)
    return jnp.concatenate([high, x - high], 0).astype(BF16)


def joined(x):
    half = x.shape[0] // 2
    return x[:half] + x[half:]


def kernel(
    grid,
    res_h, old_h, mat_h, fac_h, rig_h, coa_h, onorm_h,
    p_out, w_out, ab_out,
    resf, oldf, onorm, mat, fac, rigt, rig, rhalo, nr, coa, rows_in, rows_out, relay, cpair, cpair2, table, ubig, lin, m24,
    zb, zb2, gat, gat2, inner_o, inner_m, w_o, face_o, face_p, ret_o, ret_p, arz, arp,
    local_sem, halo_send, halo_recv, z_send, z_recv, y_send, y_recv, c_send, c_recv,
    az_send, az_recv, ap_send, ap_recv, z2_send, z2_recv, y2_send, y2_recv, c2_send, c2_recv,
):
    nz, ny, nx = grid
    count, cases, half = p_out.shape
    width = 2 * half
    ranks = rig_h.shape[0]
    own_rows = count * ranks
    taken = 8 * coa.shape[0]
    span = coa.shape[2] // CHUNKS
    per_chunk = nz // CHUNKS
    s = lax.axis_index("sub")
    g = lax.axis_index("grp")
    z, y, x, core = s // ny, s % ny, g // 2, g % 2
    groups = 2 * nx
    flat = s * groups + g
    total = nz * ny * groups
    is_first = flat == 0
    is_last = flat == total - 1

    def of_flat(i):
        return (i // groups, i % groups)

    following = of_flat((flat + 1) % total)
    previous = of_flat((flat + total - 1) % total)
    partner = (s, x * 2 + 1 - core)
    second_next = of_flat((flat + 2) % total)
    second_previous = of_flat((flat + total - 2) % total)
    beyond = of_flat((flat + total + 2 - 4 * core) % total)
    def hops(i, ring):
        return min(i, ring - i)

    steps = sorted(range(1, nz), key=lambda i: -hops(i, nz))
    line = [(((z + i) % nz) * ny + y, g) for i in steps]
    across = [(((z + i) % nz) * ny + y, x * 2 + 1 - core) for i in steps]
    offsets = [(i, j) for i in range(ny) for j in range(nx) if i or j]
    offsets = sorted(offsets, key=lambda o: -hops(o[0], ny) - hops(o[1], nx))
    plane = [(z * ny + (y + i) % ny, ((x + j) % nx) * 2 + core) for i, j in offsets]
    slot = y * nx + x

    def to(src, dst, send, recv, device):
        return pltpu.make_async_remote_copy(
            src_ref=src, dst_ref=dst, send_sem=send, recv_sem=recv,
            device_id=device, device_id_type=pl.DeviceIdType.MESH,
        )

    def tell(semaphore, device):
        pl.semaphore_signal(
            semaphore, inc=1, device_id=device, device_id_type=pl.DeviceIdType.MESH
        )

    gat2[...] = jnp.zeros_like(gat2)
    for end in (0, coa.shape[0] - 1):
        coa[end] = jnp.zeros(coa.shape[1:], F32)
    barrier = pltpu.get_barrier_semaphore()
    everyone = [*plane, *line, *across, following, previous, partner, second_next, second_previous]
    for device in everyone:
        tell(barrier, device)
    loads = [
        pltpu.make_async_copy(mat_h, mat, local_sem.at[0]),
        pltpu.make_async_copy(rig_h, rigt, local_sem.at[1]),
        pltpu.make_async_copy(res_h, resf.at[pl.ds(1, count)], local_sem.at[2]),
        pltpu.make_async_copy(old_h, oldf.at[pl.ds(1, count)], local_sem.at[3]),
        pltpu.make_async_copy(coa_h, coa.at[pl.ds(1, own_rows // 8)], local_sem.at[4]),
        pltpu.make_async_copy(fac_h, fac, local_sem.at[5]),
        pltpu.make_async_copy(onorm_h, onorm, local_sem.at[6]),
    ]
    for load in loads:
        load.start()
    ubig[...] = jnp.zeros_like(ubig)
    lin[...] = jnp.zeros_like(lin)
    rig[:, ranks:, :] = jnp.zeros((count, 8 - ranks, width), F32)

    loads[0].wait()
    unknowns = lax.broadcasted_iota(jnp.int32, (half, half), 0)
    for q in range(count):
        table[q] = jnp.where(unknowns == mat[pl.ds(q, 1), :], -1.0, 0.0).astype(BF16)
    loads[1].wait()
    for q in range(count):
        for m in range(ranks):
            rig[q, m : m + 1, :] = rigt[m, q : q + 1, :]
    for q in range(count):
        left = rig[q, :, :half]
        high = left.astype(BF16).astype(F32)
        mid = (left - high).astype(BF16).astype(F32)
        parts = jnp.concatenate([high, mid, left - high - mid], 0).astype(BF16)
        moved = mm(parts, table[q], NT)
        nr[q] = moved[:8] + moved[8:16] + moved[16:]

    rows = lax.broadcasted_iota(jnp.int32, (count * 8, LANES), 0)
    chunk = lax.broadcasted_iota(jnp.int32, (count * 8, LANES), 1) // cases
    loads[2].wait()
    resf[count] = jnp.where(is_last, 0.0, resf[count])
    rights = rig[:, :, half:].reshape(count * 8, half)
    lefts = nr[1:count].reshape((count - 1) * 8, half)
    own = resf[1:].reshape(count * cases, half)
    sums = mm(rights, own, NT, HIGHEST)
    before = mm(lefts, own, NT, HIGHEST)
    before = pltpu.roll(before, cases, 1)
    before = jnp.concatenate([jnp.zeros((8, LANES), F32), before], 0)
    sums = jnp.where(rows // 8 == chunk, sums + before, 0.0)
    sums = sums + pltpu.roll(sums, LANES // 2, 1)
    sums = sums + pltpu.roll(sums, LANES // 4, 1)
    for q in range(count):
        m24[q * ranks : (q + 1) * ranks, :] = sums[q * 8 : q * 8 + ranks]
    chunk = chunk[:8]
    tile = jnp.zeros((8, LANES), F32)
    for w in range(own_rows // 8):
        tile = jnp.where(chunk == w, m24[w * 8 : (w + 1) * 8, :], tile)
    faces = jnp.concatenate([pair(resf[count]), jnp.zeros((LANES - 2 * cases, half), BF16)], 0)
    zb[z] = tile
    loads[4].wait()
    firsts, lasts = coa[1], pltpu.roll(coa[coa.shape[0] - 2], ranks, 0)
    rows_in[...] = jnp.where(core == 1, firsts, lasts)
    rows_out[...] = jnp.where(core == 1, lasts, firsts)
    pl.semaphore_wait(barrier, len(everyone))
    edge = core * (coa.shape[0] - 1)
    some = pl.ds(0, ranks)
    halo = [
        to(res_h.at[count - 1], resf.at[0], halo_send.at[0], halo_recv.at[0], following),
        to(nr.at[0], nr.at[count], halo_send.at[1], halo_recv.at[1], previous),
        to(rig.at[count - 1, :, pl.ds(half, half)], rhalo, halo_send.at[2], halo_recv.at[2], following),
        to(old_h.at[count - 1], oldf.at[0], halo_send.at[3], halo_recv.at[3], following),
        to(rows_in.at[some], coa.at[edge, some], halo_send.at[4], halo_recv.at[4], partner),
        to(rows_out.at[some], relay.at[some], halo_send.at[5], halo_recv.at[5], partner),
    ]
    relayed = to(relay.at[some], coa.at[edge, some], halo_send.at[8], halo_recv.at[8], beyond)

    @pl.when(jnp.logical_not(is_first))
    def _():
        halo[1].start()


    def all_of(ref, number, send, recv):
        whole = ref.at[pl.ds(0, number)]
        return to(whole, whole, send, recv, partner)

    def along_line(ref, at, send, recv, devices):
        for device in devices:
            to(ref.at[at], ref.at[at], send, recv, device).start()
        return all_of(ref, len(devices), send, recv)

    def packed(ref, zl, w):
        block = jnp.zeros((8, LANES), F32)
        for a in range(CHUNKS):
            turned = ref[a * per_chunk + zl]
            if a != w:
                turned = pltpu.roll(turned, ((a - w) * cases) % LANES, 1)
            block = jnp.where(chunk == a, turned, block)
        return block

    def to_plane(ref, depth, send, recv, turn_send, turn_recv):
        def block(yx):
            return ref.at[:, yx, core, pl.ds(0, depth)]

        copies = [to(block(slot), block(slot), send, recv.at[i], d) for i, d in enumerate(plane)]
        for copy in copies:
            copy.start()
        to(block(slot), block(slot), turn_send, turn_recv, partner).start()

        def turn():
            for i in reversed(range(len(offsets))):
                dy, dx = offsets[i]
                copies[i].wait_recv()
                theirs = block(((y + ny - dy) % ny) * nx + (x + nx - dx) % nx)
                to(theirs, theirs, turn_send, turn_recv, partner).start()

        sent = ref.at[:, pl.ds(0, len(plane)), 0, pl.ds(0, depth)]
        both = ref.at[:, :, 0, pl.ds(0, depth)]
        return to(sent, sent, send, recv.at[0], partner), to(both, both, turn_send, turn_recv, partner), turn

    z_copies = along_line(zb, z, z_send, z_recv, line)
    for i in (5, 0, 3, 2, 4):
        halo[i].start()

    block = width // 4

    def forward(left, right, q):
        pairs = jnp.concatenate([mm(pair(left), table[q]).astype(BF16), pair(right)], 1)
        return jnp.concatenate(
            [
                joined(mm(pairs[:, : (i + 1) * block],
                          fac[q, i * block : (i + 1) * block, : (i + 1) * block], NT))
                for i in range(4)
            ], 1,
        )

    def backward(inner, q):
        pairs = pair(inner)
        solved = jnp.concatenate(
            [
                joined(mm(pairs[:, j * block :], fac[q, j * block :, j * block : (j + 1) * block]))
                for j in range(4)
            ], 1,
        )
        returned = joined(mm(pair(solved[:, :half]), table[q], NT))
        return solved[:, half:], returned

    def place(f, above):
        top = (2 + ranks * f if f else 0) if above else 2 + ranks * (f + 1)
        rows_of = (rhalo[:ranks] if f == 0 else rig[f - 1, :ranks, half:]) if above else nr[f, :ranks]
        if f in (0, count):
            rows_of = jnp.where(is_last if f else is_first, 0.0, rows_of)
        ubig[top : top + ranks, f * half : (f + 1) * half] = rows_of

    def keep(rows_of, values, columns):
        high = values.astype(BF16)
        low = (values - high.astype(F32)).astype(BF16)
        lin[rows_of[0] : rows_of[1], columns] = high
        lin[rows_of[0] + taken : rows_of[1] + taken, columns] = high
        lin[rows_of[0] + 2 * taken : rows_of[1] + 2 * taken, columns] = low

    def apply_all(q):
        low_row = (2 + ranks * q) // 8 * 8
        high_row = -(-(2 + ranks * (q + 3)) // 8) * 8
        sides = [
            jnp.concatenate(
                [oldf[f], resf[f], ubig[low_row:high_row, f * half : (f + 1) * half]], 0
            )
            for f in (q, q + 1)
        ]
        inner = forward(*sides, q)
        inner_o[q] = inner[:cases]
        inner_m[q] = inner[cases : 2 * cases]
        start = count * half + q * width
        keep((low_row, high_row), inner[2 * cases :], slice(start, start + width))

    for f in range(count + 1):
        if f > 0:
            place(f, True)
        if f < count:
            place(f, False)
    loads[3].wait()
    oldf[count] = jnp.where(is_last, 0.0, oldf[count])
    loads[5].wait()
    apply_all(1)
    halo[5].wait_recv()
    relayed.start()
    for q in range(2, count - 1):
        apply_all(q)

    def send_corrections():
        @pl.when(jnp.logical_not(is_last))
        def _():
            halo[1].wait_recv()

        added = mm(pair(jnp.where(is_last, 0.0, nr[count])), faces, NT)
        added = added[:8] + pltpu.roll(added[:8], LANES - cases, 1) + added[8:]
        zb2[z] = jnp.where(chunk == 0, added, 0.0)
        for device in line:
            to(zb2.at[z], zb2.at[z], z2_send, z2_recv, device).start()

    far_next = jnp.logical_and(jnp.logical_and(x == nx - 1, y == ny - 1), core == 1)
    pl.when(jnp.logical_not(far_next))(send_corrections)
    z_copies.wait()
    for zl in range(per_chunk):
        for w in range(own_rows // 8):
            gat[zl, slot, core, w * 8 : (w + 1) * 8, :] = packed(zb, zl, w)
    y_copies, c_copies, turn = to_plane(gat, own_rows, y_send, y_recv, c_send, c_recv)
    pl.when(far_next)(send_corrections)
    def take_back(q):
        solved, returned = backward(inner_o[q], q)
        w_o[q] = solved if q else solved + w_o[0]
        if q == 1:
            w_o[0] = returned
        elif q:
            w_o[q - 1] += returned
        else:
            ret_o[...] = returned

    for q in range(1, count - 1):
        take_back(q)
    all_of(zb2, len(line), z2_send, z2_recv).wait()
    for zl in range(per_chunk):
        gat2[zl, slot, core, :ranks] = packed(zb2, zl, 0)[:ranks]
    y2_copies, c2_copies, turn2 = to_plane(gat2, ranks, y2_send, y2_recv, c2_send, c2_recv)
    halo[0].wait_recv()
    halo[2].wait_recv()
    halo[3].wait_recv()
    resf[0] = jnp.where(is_first, 0.0, resf[0])
    place(0, True)
    place(count, False)
    oldf[0] = jnp.where(is_first, 0.0, oldf[0])
    for q in (0, count - 1):
        apply_all(q)
    keep((0, taken), ubig[:, half:], slice(0, count * half))
    take_back(0)
    ret_o_copy = to(ret_o, face_o, halo_send.at[6], halo_recv.at[6], previous)
    ret_o_copy.start()
    take_back(count - 1)
    halo[4].wait_recv()
    relayed.wait_recv()
    period = min(LANES // 8 * own_rows, span)
    kept = period // own_rows * 8
    source = lax.broadcasted_iota(jnp.int32, (period, kept), 0)
    target = lax.broadcasted_iota(jnp.int32, (period, kept), 1)
    chosen = jnp.where(source == target // 8 * own_rows + target % 8, 1.0, 0.0).astype(BF16)
    coarse_rows = coa[...].reshape(taken, CHUNKS * span)
    following_rows = pltpu.roll(coarse_rows, CHUNKS * span - own_rows, 1)
    for a in range(CHUNKS):
        part = slice(a * span, (a + 1) * span)
        rows_of = slice(a * 2 * taken, (a + 1) * 2 * taken)
        cpair[rows_of] = pair(coarse_rows[:, part])
        shifted = pair(following_rows[:, part])
        cpair2[rows_of] = jnp.concatenate(
            [mm(shifted[:, k : k + period], chosen) for k in range(0, span, period)], 1
        ).astype(BF16)

    turn()
    turn2()
    c_copies.wait_recv()

    def product(rows_of, gathered):
        high = gathered.astype(BF16)
        low = (gathered - high.astype(F32)).astype(BF16)
        both = mm(rows_of[...], jnp.concatenate([high, low], 1))
        return both[:, :LANES] + both[:, LANES:]

    products = product(cpair, gat[...].reshape(span, LANES))
    c2_copies.wait_recv()
    products = products + product(cpair2, gat2[...].reshape(span // own_rows * 8, LANES))
    chunk_all = lax.broadcasted_iota(jnp.int32, (taken, LANES), 1) // cases
    coeffs = jnp.zeros((taken, LANES), F32)
    for a in range(CHUNKS):
        coeffs = jnp.where(chunk_all == a, joined(products[a * 2 * taken : (a + 1) * 2 * taken]), coeffs)
    coeffs = coeffs + pltpu.roll(coeffs, LANES // 2, 1)
    coeffs = coeffs + pltpu.roll(coeffs, LANES // 4, 1)
    high = coeffs.astype(BF16).astype(F32)
    thrice = jnp.concatenate(
        [high, coeffs - high, high, jnp.zeros((LANES - 3 * taken, LANES), F32)], 0
    ).T[:cases].astype(BF16)
    moved = mm(thrice, lin[...])
    norms, pp, po, oo = (jnp.zeros((cases, 1), F32) for _ in range(4))
    inners = []
    for q in range(count):
        part = resf[q + 1] - moved[:, q * half : (q + 1) * half]
        p_out[q] = part
        start = count * half + q * width
        inner = inner_m[q] - moved[:, start : start + width]
        inners.append(inner)
        old_inner = inner_o[q]
        norms = norms + jnp.sum(part * part, 1, keepdims=True)
        pp = pp + jnp.sum(inner * inner, 1, keepdims=True)
        po = po + jnp.sum(inner * old_inner, 1, keepdims=True)
        oo = oo + jnp.sum(old_inner * old_inner, 1, keepdims=True)

    lane = lax.broadcasted_iota(jnp.int32, (cases, LANES), 1)
    square = jnp.zeros((cases, LANES), F32)
    for i, column in enumerate((norms, pp, po, oo)):
        square = jnp.where(lane == i, column, square)
    square = jnp.concatenate([square, jnp.zeros((LANES - cases, LANES), F32)], 0).T
    here = 2 * z + core
    arz[here] = square[0:1] + sum(pltpu.roll(square[i : i + 1], i * cases, 1) for i in range(1, CHUNKS))
    pairs_of = [device for both in zip(line, across) for device in both]
    az_copies = along_line(arz, here, az_send, az_recv, [*pairs_of, partner])

    for q in range(count):
        solved, returned = backward(inners[q], q)
        w_out[q] = solved
        if q:
            w_out[q - 1] += returned
        else:
            ret_p[...] = returned
            ret_p_copy = to(ret_p, face_p, halo_send.at[7], halo_recv.at[7], previous)
            ret_p_copy.start()
    az_copies.wait()
    arp[slot] = sum(arz[i] for i in range(2 * nz))
    ap_copies = along_line(arp, slot, ap_send, ap_recv, plane)
    loads[6].wait()
    ret_o_copy.wait()
    ret_p_copy.wait()
    w_o[count - 1] = jnp.where(is_last, 0.0, w_o[count - 1] + face_o[...])
    w_out[count - 1] = jnp.where(is_last, 0.0, w_out[count - 1] + face_p[...])
    @pl.when(jnp.logical_not(is_first))
    def _():
        halo[1].wait_send()

    for copy in (halo[0], *halo[2:], relayed, y_copies, c_copies, y2_copies, c2_copies):
        copy.wait_send()
    ap_copies.wait()
    totals = sum(arp[i] for i in range(ny * nx))
    norm, pure, mixed, old_part = (pltpu.roll(totals, (-i * cases) % LANES, 1) if i else totals for i in range(CHUNKS))
    beta = norm / jnp.concatenate([onorm[...], jnp.ones((1, LANES - cases), F32)], 1)
    curvature = pure + 2.0 * beta * mixed + beta * beta * old_part
    alpha = norm / curvature
    row = lax.broadcasted_iota(jnp.int32, (LANES, LANES), 0)
    square = jnp.where(row == 0, beta, jnp.where(row == 1, alpha, 0.0)).T
    ab_out[0] = jnp.broadcast_to(square[:cases, 0:1], (cases, half))
    ab_out[1] = jnp.broadcast_to(square[:cases, 1:2], (cases, half))
    column = square[:cases, 0:1]
    for q in range(count):
        w_out[q] += column * w_o[q]


def solution(mesh, ny=4):
    nz, nx = mesh.shape["sub"] // ny, mesh.shape["grp"] // 2
    both = ("sub", "grp")

    def on_device(multipliers, residual, old_direction, old_norms, matching, factor_inverse, rigid_modes, coarse_inverse):
        count, cases, half = multipliers.shape
        ranks = rigid_modes.shape[1]
        own_rows = count * ranks
        width = 2 * half
        coarse = coarse_inverse.shape[1]
        field = jax.ShapeDtypeStruct((count, cases, half), F32)
        dma = pltpu.SemaphoreType.DMA
        taken = own_rows + 16
        vmem = pltpu.VMEM
        scratch = [
            vmem((count + 1, cases, half), F32),
            vmem((count + 1, cases, half), F32),
            vmem((1, cases), F32),
            vmem((count, half), jnp.int32),
            vmem((count, width, width), BF16),
            vmem((ranks, count, width), F32),
            vmem((count, 8, width), F32),
            vmem((8, half), F32),
            vmem((count + 1, 8, half), F32),
            vmem((taken // 8, 8, coarse), F32),
            vmem((8, coarse), F32),
            vmem((8, coarse), F32),
            vmem((8, coarse), F32),
            vmem((2 * CHUNKS * taken, coarse // CHUNKS), BF16),
            vmem((2 * CHUNKS * taken, coarse // CHUNKS // own_rows * 8), BF16),
            vmem((count, half, half), BF16),
            vmem((taken, (count + 1) * half), F32),
            vmem((LANES, count * (half + width)), BF16),
            vmem((own_rows, LANES), F32),
            vmem((nz, 8, LANES), F32),
            vmem((nz, 8, LANES), F32),
            vmem((nz // CHUNKS, ny * nx, 2, own_rows, LANES), F32),
            vmem((nz // CHUNKS, ny * nx, 2, 8, LANES), F32),
            vmem((count, cases, width), F32),
            vmem((count, cases, width), F32),
            vmem((count, cases, half), F32),
            vmem((cases, half), F32),
            vmem((cases, half), F32),
            vmem((cases, half), F32),
            vmem((cases, half), F32),
            vmem((2 * nz, 1, LANES), F32),
            vmem((ny * nx, 1, LANES), F32),
            dma((7,)), dma((9,)), dma((9,)),
            dma, dma, dma, dma((ny * nx - 1,)), dma, dma,
            dma, dma, dma, dma,
            dma, dma, dma, dma((ny * nx - 1,)), dma, dma,
        ]
        projected, image, steps = pl.pallas_call(
            functools.partial(kernel, (nz, ny, nx)),
            out_shape=(field, field, jax.ShapeDtypeStruct((2, cases, half), F32)),
            in_specs=[pl.BlockSpec(memory_space=pltpu.HBM)] * 7,
            out_specs=(pl.BlockSpec(memory_space=pltpu.VMEM),) * 3,
            scratch_shapes=scratch,
            compiler_params=pltpu.CompilerParams(
                collective_id=0, has_side_effects=True, vmem_limit_bytes=48 << 20
            ),
        )(*(pltpu.with_memory_space_constraint(a, pltpu.HBM) for a in (residual, old_direction, matching, factor_inverse, rigid_modes.transpose(1, 0, 2), coarse_inverse.reshape(own_rows // 8, 8, coarse), old_norms[None])))
        flat = lax.axis_index(both) * count + jnp.arange(count, dtype=jnp.int32)
        retain = (flat != count * lax.axis_size(both) - 1).astype(F32)[:, None, None]
        beta, alpha = steps[0:1], steps[1:2]
        direction = projected + beta * old_direction * retain
        return multipliers + alpha * direction, residual * retain - alpha * image, direction

    fields = P(both, None, None)
    return jax.shard_map(
        on_device,
        mesh=mesh,
        in_specs=(fields, fields, fields, P(), P(both, None), fields, fields, P(both, None)),
        out_specs=(fields, fields, fields),
        check_vma=False,
    )
```

```python
import functools

import jax
import jax.numpy as jnp
from jax import lax
from jax.experimental import pallas as pl
from jax.experimental.pallas import tpu as pltpu
from jax.sharding import PartitionSpec as P

F32 = jnp.float32
BF16 = jnp.bfloat16
HIGHEST = lax.Precision.HIGHEST
CHUNKS = 4
LANES = 128
NN = (((1,), (0,)), ((), ()))
NT = (((1,), (1,)), ((), ()))


def mm(a, b, dims=NN, precision=None):
    return lax.dot_general(a, b, dims, precision=precision, preferred_element_type=F32)


def pair(x):
    high = x.astype(BF16).astype(F32)
    return jnp.concatenate([high, x - high], 0).astype(BF16)


def joined(x):
    half = x.shape[0] // 2
    return x[:half] + x[half:]


def kernel(
    grid,
    res_h, old_h, mat_h, fac_h, rig_h, coa_h, onorm_h,
    p_out, w_out, ab_out,
    resf, oldf, onorm, mat, fac, rigt, rig, rhalo, nr, coa, rows_in, rows_out, relay, cpair, cpair2, table, ubig, lin, m24,
    zb, zb2, gat, gat2, inner_o, inner_m, w_o, face_o, face_p, ret_o, ret_p, arz, arp,
    local_sem, halo_send, halo_recv, z_send, z_recv, y_send, y_recv, c_send, c_recv,
    az_send, az_recv, ap_send, ap_recv, z2_send, z2_recv, y2_send, y2_recv, c2_send, c2_recv,
):
    nz, ny, nx = grid
    count, cases, half = p_out.shape
    width = 2 * half
    ranks = rig_h.shape[0]
    own_rows = count * ranks
    taken = 8 * coa.shape[0]
    span = coa.shape[2] // CHUNKS
    per_chunk = nz // CHUNKS
    s = lax.axis_index("sub")
    g = lax.axis_index("grp")
    z, y, x, core = s // ny, s % ny, g // 2, g % 2
    groups = 2 * nx
    flat = s * groups + g
    total = nz * ny * groups
    is_first = flat == 0
    is_last = flat == total - 1

    def of_flat(i):
        return (i // groups, i % groups)

    following = of_flat((flat + 1) % total)
    previous = of_flat((flat + total - 1) % total)
    partner = (s, x * 2 + 1 - core)
    second_next = of_flat((flat + 2) % total)
    second_previous = of_flat((flat + total - 2) % total)
    beyond = of_flat((flat + total + 2 - 4 * core) % total)
    def hops(i, ring):
        return min(i, ring - i)

    steps = sorted(range(1, nz), key=lambda i: -hops(i, nz))
    line = [(((z + i) % nz) * ny + y, g) for i in steps]
    across = [(((z + i) % nz) * ny + y, x * 2 + 1 - core) for i in steps]
    offsets = [(i, j) for i in range(ny) for j in range(nx) if i or j]
    offsets = sorted(offsets, key=lambda o: -hops(o[0], ny) - hops(o[1], nx))
    rings = [hops(i, ny) + hops(j, nx) for i, j in offsets]
    plane = [(z * ny + (y + i) % ny, ((x + j) % nx) * 2 + core) for i, j in offsets]
    slot = y * nx + x

    def to(src, dst, send, recv, device):
        return pltpu.make_async_remote_copy(
            src_ref=src, dst_ref=dst, send_sem=send, recv_sem=recv,
            device_id=device, device_id_type=pl.DeviceIdType.MESH,
        )

    def tell(semaphore, device):
        pl.semaphore_signal(
            semaphore, inc=1, device_id=device, device_id_type=pl.DeviceIdType.MESH
        )

    gat2[...] = jnp.zeros_like(gat2)
    for end in (0, coa.shape[0] - 1):
        coa[end] = jnp.zeros(coa.shape[1:], F32)
    barrier = pltpu.get_barrier_semaphore()
    everyone = [*plane, *line, *across, following, previous, partner, second_next, second_previous]
    for device in everyone:
        tell(barrier, device)
    loads = [
        pltpu.make_async_copy(mat_h, mat, local_sem.at[0]),
        pltpu.make_async_copy(rig_h, rigt, local_sem.at[1]),
        pltpu.make_async_copy(res_h, resf.at[pl.ds(1, count)], local_sem.at[2]),
        pltpu.make_async_copy(old_h, oldf.at[pl.ds(1, count)], local_sem.at[3]),
        pltpu.make_async_copy(coa_h, coa.at[pl.ds(1, own_rows // 8)], local_sem.at[4]),
        pltpu.make_async_copy(fac_h, fac, local_sem.at[5]),
        pltpu.make_async_copy(onorm_h, onorm, local_sem.at[6]),
    ]
    for load in loads:
        load.start()
    ubig[...] = jnp.zeros_like(ubig)
    lin[...] = jnp.zeros_like(lin)
    rig[:, ranks:, :] = jnp.zeros((count, 8 - ranks, width), F32)

    loads[0].wait()
    unknowns = lax.broadcasted_iota(jnp.int32, (half, half), 0)
    for q in range(count):
        table[q] = jnp.where(unknowns == mat[pl.ds(q, 1), :], -1.0, 0.0).astype(BF16)
    loads[1].wait()
    for q in range(count):
        for m in range(ranks):
            rig[q, m : m + 1, :] = rigt[m, q : q + 1, :]
    for q in range(count):
        left = rig[q, :, :half]
        high = left.astype(BF16).astype(F32)
        mid = (left - high).astype(BF16).astype(F32)
        parts = jnp.concatenate([high, mid, left - high - mid], 0).astype(BF16)
        moved = mm(parts, table[q], NT)
        nr[q] = moved[:8] + moved[8:16] + moved[16:]

    rows = lax.broadcasted_iota(jnp.int32, (count * 8, LANES), 0)
    chunk = lax.broadcasted_iota(jnp.int32, (count * 8, LANES), 1) // cases
    loads[2].wait()
    resf[count] = jnp.where(is_last, 0.0, resf[count])
    rights = rig[:, :, half:].reshape(count * 8, half)
    lefts = nr[1:count].reshape((count - 1) * 8, half)
    own = resf[1:].reshape(count * cases, half)
    sums = mm(rights, own, NT, HIGHEST)
    before = mm(lefts, own, NT, HIGHEST)
    before = pltpu.roll(before, cases, 1)
    before = jnp.concatenate([jnp.zeros((8, LANES), F32), before], 0)
    sums = jnp.where(rows // 8 == chunk, sums + before, 0.0)
    sums = sums + pltpu.roll(sums, LANES // 2, 1)
    sums = sums + pltpu.roll(sums, LANES // 4, 1)
    for q in range(count):
        m24[q * ranks : (q + 1) * ranks, :] = sums[q * 8 : q * 8 + ranks]
    chunk = chunk[:8]
    tile = jnp.zeros((8, LANES), F32)
    for w in range(own_rows // 8):
        tile = jnp.where(chunk == w, m24[w * 8 : (w + 1) * 8, :], tile)
    faces = jnp.concatenate([pair(resf[count]), jnp.zeros((LANES - 2 * cases, half), BF16)], 0)
    zb[z] = tile
    loads[4].wait()
    firsts, lasts = coa[1], pltpu.roll(coa[coa.shape[0] - 2], ranks, 0)
    rows_in[...] = jnp.where(core == 1, firsts, lasts)
    rows_out[...] = jnp.where(core == 1, lasts, firsts)
    pl.semaphore_wait(barrier, len(everyone))
    edge = core * (coa.shape[0] - 1)
    some = pl.ds(0, ranks)
    halo = [
        to(res_h.at[count - 1], resf.at[0], halo_send.at[0], halo_recv.at[0], following),
        to(nr.at[0], nr.at[count], halo_send.at[1], halo_recv.at[1], previous),
        to(rig.at[count - 1, :, pl.ds(half, half)], rhalo, halo_send.at[2], halo_recv.at[2], following),
        to(old_h.at[count - 1], oldf.at[0], halo_send.at[3], halo_recv.at[3], following),
        to(rows_in.at[some], coa.at[edge, some], halo_send.at[4], halo_recv.at[4], partner),
        to(rows_out.at[some], relay.at[some], halo_send.at[5], halo_recv.at[5], partner),
    ]
    relayed = to(relay.at[some], coa.at[edge, some], halo_send.at[8], halo_recv.at[8], beyond)

    @pl.when(jnp.logical_not(is_first))
    def _():
        halo[1].start()


    def all_of(ref, number, send, recv):
        whole = ref.at[pl.ds(0, number)]
        return to(whole, whole, send, recv, partner)

    def along_line(ref, at, send, recv, devices):
        for device in devices:
            to(ref.at[at], ref.at[at], send, recv, device).start()
        return all_of(ref, len(devices), send, recv)

    def packed(ref, zl, w):
        block = jnp.zeros((8, LANES), F32)
        for a in range(CHUNKS):
            turned = ref[a * per_chunk + zl]
            if a != w:
                turned = pltpu.roll(turned, ((a - w) * cases) % LANES, 1)
            block = jnp.where(chunk == a, turned, block)
        return block

    def to_plane(ref, depth, send, recv, turn_send, turn_recv):
        def block(yx):
            return ref.at[:, yx, core, pl.ds(0, depth)]

        for device, ring in zip(plane, rings):
            to(block(slot), block(slot), send, recv.at[ring - 1], device).start()
        to(block(slot), block(slot), turn_send, turn_recv, partner).start()

        def turn():
            for ring in sorted(set(rings)):
                members = [o for o, r in zip(offsets, rings) if r == ring]
                group = ref.at[:, pl.ds(0, len(members)), 0, pl.ds(0, depth)]
                to(group, group, send, recv.at[ring - 1], partner).wait_recv()
                for dy, dx in members:
                    theirs = block(((y + ny - dy) % ny) * nx + (x + nx - dx) % nx)
                    to(theirs, theirs, turn_send, turn_recv, partner).start()

        sent = ref.at[:, pl.ds(0, len(plane)), 0, pl.ds(0, depth)]
        both = ref.at[:, :, 0, pl.ds(0, depth)]
        return to(sent, sent, send, recv.at[0], partner), to(both, both, turn_send, turn_recv, partner), turn

    z_copies = along_line(zb, z, z_send, z_recv, line)
    for i in (5, 0, 3, 2, 4):
        halo[i].start()

    block = width // 4

    def forward(left, right, q):
        pairs = jnp.concatenate([mm(pair(left), table[q]).astype(BF16), pair(right)], 1)
        return jnp.concatenate(
            [
                joined(mm(pairs[:, : (i + 1) * block],
                          fac[q, i * block : (i + 1) * block, : (i + 1) * block], NT))
                for i in range(4)
            ], 1,
        )

    def backward(inner, q):
        pairs = pair(inner)
        solved = jnp.concatenate(
            [
                joined(mm(pairs[:, j * block :], fac[q, j * block :, j * block : (j + 1) * block]))
                for j in range(4)
            ], 1,
        )
        returned = joined(mm(pair(solved[:, :half]), table[q], NT))
        return solved[:, half:], returned

    def place(f, above):
        top = (2 + ranks * f if f else 0) if above else 2 + ranks * (f + 1)
        rows_of = (rhalo[:ranks] if f == 0 else rig[f - 1, :ranks, half:]) if above else nr[f, :ranks]
        if f in (0, count):
            rows_of = jnp.where(is_last if f else is_first, 0.0, rows_of)
        ubig[top : top + ranks, f * half : (f + 1) * half] = rows_of

    def keep(rows_of, values, columns):
        high = values.astype(BF16)
        low = (values - high.astype(F32)).astype(BF16)
        lin[rows_of[0] : rows_of[1], columns] = high
        lin[rows_of[0] + taken : rows_of[1] + taken, columns] = high
        lin[rows_of[0] + 2 * taken : rows_of[1] + 2 * taken, columns] = low

    def apply_all(q):
        low_row = (2 + ranks * q) // 8 * 8
        high_row = -(-(2 + ranks * (q + 3)) // 8) * 8
        sides = [
            jnp.concatenate(
                [oldf[f], resf[f], ubig[low_row:high_row, f * half : (f + 1) * half]], 0
            )
            for f in (q, q + 1)
        ]
        inner = forward(*sides, q)
        inner_o[q] = inner[:cases]
        inner_m[q] = inner[cases : 2 * cases]
        start = count * half + q * width
        keep((low_row, high_row), inner[2 * cases :], slice(start, start + width))

    for f in range(count + 1):
        if f > 0:
            place(f, True)
        if f < count:
            place(f, False)
    loads[3].wait()
    oldf[count] = jnp.where(is_last, 0.0, oldf[count])
    loads[5].wait()
    apply_all(1)
    halo[5].wait_recv()
    relayed.start()
    for q in range(2, count - 1):
        apply_all(q)

    def send_corrections():
        @pl.when(jnp.logical_not(is_last))
        def _():
            halo[1].wait_recv()

        added = mm(pair(jnp.where(is_last, 0.0, nr[count])), faces, NT)
        added = added[:8] + pltpu.roll(added[:8], LANES - cases, 1) + added[8:]
        zb2[z] = jnp.where(chunk == 0, added, 0.0)
        for device in line:
            to(zb2.at[z], zb2.at[z], z2_send, z2_recv, device).start()

    far_next = jnp.logical_and(jnp.logical_and(x == nx - 1, y == ny - 1), core == 1)
    pl.when(jnp.logical_not(far_next))(send_corrections)
    z_copies.wait()
    for zl in range(per_chunk):
        for w in range(own_rows // 8):
            gat[zl, slot, core, w * 8 : (w + 1) * 8, :] = packed(zb, zl, w)
    y_copies, c_copies, turn = to_plane(gat, own_rows, y_send, y_recv, c_send, c_recv)
    pl.when(far_next)(send_corrections)
    def take_back(q):
        solved, returned = backward(inner_o[q], q)
        w_o[q] = solved if q else solved + w_o[0]
        if q == 1:
            w_o[0] = returned
        elif q:
            w_o[q - 1] += returned
        else:
            ret_o[...] = returned

    for q in range(1, count - 1):
        take_back(q)
    all_of(zb2, len(line), z2_send, z2_recv).wait()
    for zl in range(per_chunk):
        gat2[zl, slot, core, :ranks] = packed(zb2, zl, 0)[:ranks]
    y2_copies, c2_copies, turn2 = to_plane(gat2, ranks, y2_send, y2_recv, c2_send, c2_recv)
    halo[0].wait_recv()
    halo[2].wait_recv()
    halo[3].wait_recv()
    resf[0] = jnp.where(is_first, 0.0, resf[0])
    place(0, True)
    place(count, False)
    oldf[0] = jnp.where(is_first, 0.0, oldf[0])
    for q in (0, count - 1):
        apply_all(q)
    keep((0, taken), ubig[:, half:], slice(0, count * half))
    take_back(0)
    ret_o_copy = to(ret_o, face_o, halo_send.at[6], halo_recv.at[6], previous)
    ret_o_copy.start()
    take_back(count - 1)
    turn()
    halo[4].wait_recv()
    relayed.wait_recv()
    period = min(LANES // 8 * own_rows, span)
    kept = period // own_rows * 8
    source = lax.broadcasted_iota(jnp.int32, (period, kept), 0)
    target = lax.broadcasted_iota(jnp.int32, (period, kept), 1)
    chosen = jnp.where(source == target // 8 * own_rows + target % 8, 1.0, 0.0).astype(BF16)
    coarse_rows = coa[...].reshape(taken, CHUNKS * span)
    following_rows = pltpu.roll(coarse_rows, CHUNKS * span - own_rows, 1)
    for a in range(CHUNKS):
        part = slice(a * span, (a + 1) * span)
        rows_of = slice(a * 2 * taken, (a + 1) * 2 * taken)
        cpair[rows_of] = pair(coarse_rows[:, part])
        shifted = pair(following_rows[:, part])
        cpair2[rows_of] = jnp.concatenate(
            [mm(shifted[:, k : k + period], chosen) for k in range(0, span, period)], 1
        ).astype(BF16)

    turn2()
    c_copies.wait_recv()

    def product(rows_of, gathered):
        high = gathered.astype(BF16)
        low = (gathered - high.astype(F32)).astype(BF16)
        both = mm(rows_of[...], jnp.concatenate([high, low], 1))
        return both[:, :LANES] + both[:, LANES:]

    products = product(cpair, gat[...].reshape(span, LANES))
    c2_copies.wait_recv()
    products = products + product(cpair2, gat2[...].reshape(span // own_rows * 8, LANES))
    chunk_all = lax.broadcasted_iota(jnp.int32, (taken, LANES), 1) // cases
    coeffs = jnp.zeros((taken, LANES), F32)
    for a in range(CHUNKS):
        coeffs = jnp.where(chunk_all == a, joined(products[a * 2 * taken : (a + 1) * 2 * taken]), coeffs)
    coeffs = coeffs + pltpu.roll(coeffs, LANES // 2, 1)
    coeffs = coeffs + pltpu.roll(coeffs, LANES // 4, 1)
    high = coeffs.astype(BF16).astype(F32)
    thrice = jnp.concatenate(
        [high, coeffs - high, high, jnp.zeros((LANES - 3 * taken, LANES), F32)], 0
    ).T[:cases].astype(BF16)
    moved = mm(thrice, lin[...])
    norms, pp, po, oo = (jnp.zeros((cases, 1), F32) for _ in range(4))
    inners = []
    for q in range(count):
        part = resf[q + 1] - moved[:, q * half : (q + 1) * half]
        p_out[q] = part
        start = count * half + q * width
        inner = inner_m[q] - moved[:, start : start + width]
        inners.append(inner)
        old_inner = inner_o[q]
        norms = norms + jnp.sum(part * part, 1, keepdims=True)
        pp = pp + jnp.sum(inner * inner, 1, keepdims=True)
        po = po + jnp.sum(inner * old_inner, 1, keepdims=True)
        oo = oo + jnp.sum(old_inner * old_inner, 1, keepdims=True)

    lane = lax.broadcasted_iota(jnp.int32, (cases, LANES), 1)
    square = jnp.zeros((cases, LANES), F32)
    for i, column in enumerate((norms, pp, po, oo)):
        square = jnp.where(lane == i, column, square)
    square = jnp.concatenate([square, jnp.zeros((LANES - cases, LANES), F32)], 0).T
    here = 2 * z + core
    arz[here] = square[0:1] + sum(pltpu.roll(square[i : i + 1], i * cases, 1) for i in range(1, CHUNKS))
    pairs_of = [device for both in zip(line, across) for device in both]
    az_copies = along_line(arz, here, az_send, az_recv, [*pairs_of, partner])

    for q in range(count):
        solved, returned = backward(inners[q], q)
        w_out[q] = solved
        if q:
            w_out[q - 1] += returned
        else:
            ret_p[...] = returned
            ret_p_copy = to(ret_p, face_p, halo_send.at[7], halo_recv.at[7], previous)
            ret_p_copy.start()
    az_copies.wait()
    arp[slot] = sum(arz[i] for i in range(2 * nz))
    ap_copies = along_line(arp, slot, ap_send, ap_recv, plane)
    loads[6].wait()
    ret_o_copy.wait()
    ret_p_copy.wait()
    w_o[count - 1] = jnp.where(is_last, 0.0, w_o[count - 1] + face_o[...])
    w_out[count - 1] = jnp.where(is_last, 0.0, w_out[count - 1] + face_p[...])
    @pl.when(jnp.logical_not(is_first))
    def _():
        halo[1].wait_send()

    for copy in (halo[0], *halo[2:], relayed, y_copies, c_copies, y2_copies, c2_copies):
        copy.wait_send()
    ap_copies.wait()
    totals = sum(arp[i] for i in range(ny * nx))
    norm, pure, mixed, old_part = (pltpu.roll(totals, (-i * cases) % LANES, 1) if i else totals for i in range(CHUNKS))
    beta = norm / jnp.concatenate([onorm[...], jnp.ones((1, LANES - cases), F32)], 1)
    curvature = pure + 2.0 * beta * mixed + beta * beta * old_part
    alpha = norm / curvature
    row = lax.broadcasted_iota(jnp.int32, (LANES, LANES), 0)
    square = jnp.where(row == 0, beta, jnp.where(row == 1, alpha, 0.0)).T
    ab_out[0] = jnp.broadcast_to(square[:cases, 0:1], (cases, half))
    ab_out[1] = jnp.broadcast_to(square[:cases, 1:2], (cases, half))
    column = square[:cases, 0:1]
    for q in range(count):
        w_out[q] += column * w_o[q]


def solution(mesh, ny=4):
    nz, nx = mesh.shape["sub"] // ny, mesh.shape["grp"] // 2
    both = ("sub", "grp")

    def on_device(multipliers, residual, old_direction, old_norms, matching, factor_inverse, rigid_modes, coarse_inverse):
        count, cases, half = multipliers.shape
        ranks = rigid_modes.shape[1]
        own_rows = count * ranks
        width = 2 * half
        coarse = coarse_inverse.shape[1]
        field = jax.ShapeDtypeStruct((count, cases, half), F32)
        dma = pltpu.SemaphoreType.DMA
        taken = own_rows + 16
        vmem = pltpu.VMEM
        scratch = [
            vmem((count + 1, cases, half), F32),
            vmem((count + 1, cases, half), F32),
            vmem((1, cases), F32),
            vmem((count, half), jnp.int32),
            vmem((count, width, width), BF16),
            vmem((ranks, count, width), F32),
            vmem((count, 8, width), F32),
            vmem((8, half), F32),
            vmem((count + 1, 8, half), F32),
            vmem((taken // 8, 8, coarse), F32),
            vmem((8, coarse), F32),
            vmem((8, coarse), F32),
            vmem((8, coarse), F32),
            vmem((2 * CHUNKS * taken, coarse // CHUNKS), BF16),
            vmem((2 * CHUNKS * taken, coarse // CHUNKS // own_rows * 8), BF16),
            vmem((count, half, half), BF16),
            vmem((taken, (count + 1) * half), F32),
            vmem((LANES, count * (half + width)), BF16),
            vmem((own_rows, LANES), F32),
            vmem((nz, 8, LANES), F32),
            vmem((nz, 8, LANES), F32),
            vmem((nz // CHUNKS, ny * nx, 2, own_rows, LANES), F32),
            vmem((nz // CHUNKS, ny * nx, 2, 8, LANES), F32),
            vmem((count, cases, width), F32),
            vmem((count, cases, width), F32),
            vmem((count, cases, half), F32),
            vmem((cases, half), F32),
            vmem((cases, half), F32),
            vmem((cases, half), F32),
            vmem((cases, half), F32),
            vmem((2 * nz, 1, LANES), F32),
            vmem((ny * nx, 1, LANES), F32),
            dma((7,)), dma((9,)), dma((9,)),
            dma, dma, dma, dma((ny // 2 + nx // 2,)), dma, dma,
            dma, dma, dma, dma,
            dma, dma, dma, dma((ny // 2 + nx // 2,)), dma, dma,
        ]
        projected, image, steps = pl.pallas_call(
            functools.partial(kernel, (nz, ny, nx)),
            out_shape=(field, field, jax.ShapeDtypeStruct((2, cases, half), F32)),
            in_specs=[pl.BlockSpec(memory_space=pltpu.HBM)] * 7,
            out_specs=(pl.BlockSpec(memory_space=pltpu.VMEM),) * 3,
            scratch_shapes=scratch,
            compiler_params=pltpu.CompilerParams(
                collective_id=0, has_side_effects=True, vmem_limit_bytes=48 << 20
            ),
        )(*(pltpu.with_memory_space_constraint(a, pltpu.HBM) for a in (residual, old_direction, matching, factor_inverse, rigid_modes.transpose(1, 0, 2), coarse_inverse.reshape(own_rows // 8, 8, coarse), old_norms[None])))
        flat = lax.axis_index(both) * count + jnp.arange(count, dtype=jnp.int32)
        retain = (flat != count * lax.axis_size(both) - 1).astype(F32)[:, None, None]
        beta, alpha = steps[0:1], steps[1:2]
        direction = projected + beta * old_direction * retain
        return multipliers + alpha * direction, residual * retain - alpha * image, direction

    fields = P(both, None, None)
    return jax.shard_map(
        on_device,
        mesh=mesh,
        in_specs=(fields, fields, fields, P(), P(both, None), fields, fields, P(both, None)),
        out_specs=(fields, fields, fields),
        check_vma=False,
    )
```

```python
import functools

import jax
import jax.numpy as jnp
from jax import lax
from jax.experimental import pallas as pl
from jax.experimental.pallas import tpu as pltpu
from jax.sharding import PartitionSpec as P

F32 = jnp.float32
BF16 = jnp.bfloat16
HIGHEST = lax.Precision.HIGHEST
CHUNKS = 4
LANES = 128
NN = (((1,), (0,)), ((), ()))
NT = (((1,), (1,)), ((), ()))


def mm(a, b, dims=NN, precision=None):
    return lax.dot_general(a, b, dims, precision=precision, preferred_element_type=F32)


def pair(x):
    high = x.astype(BF16).astype(F32)
    return jnp.concatenate([high, x - high], 0).astype(BF16)


def joined(x):
    half = x.shape[0] // 2
    return x[:half] + x[half:]


def kernel(
    grid,
    res_h, old_h, mat_h, fac_h, rig_h, coa_h, onorm_h,
    p_out, w_out, ab_out,
    resf, oldf, onorm, mat, fac, rigt, rig, rhalo, nr, coa, rows_in, rows_out, relay, cpair, cpair2, table, ubig, lin, m24,
    zb, zb2, gat, gat2, inner_o, inner_m, w_o, face_o, face_p, ret_o, ret_p, arz, arp,
    local_sem, halo_send, halo_recv, z_send, z_recv, y_send, y_recv, c_send, c_recv,
    az_recv, ap_recv, z2_send, z2_recv, y2_send, y2_recv, c2_send, c2_recv,
):
    nz, ny, nx = grid
    count, cases, half = p_out.shape
    width = 2 * half
    ranks = rig_h.shape[0]
    own_rows = count * ranks
    taken = 8 * coa.shape[0]
    span = coa.shape[2] // CHUNKS
    per_chunk = nz // CHUNKS
    s = lax.axis_index("sub")
    g = lax.axis_index("grp")
    z, y, x, core = s // ny, s % ny, g // 2, g % 2
    groups = 2 * nx
    flat = s * groups + g
    total = nz * ny * groups
    is_first = flat == 0
    is_last = flat == total - 1

    def of_flat(i):
        return (i // groups, i % groups)

    following = of_flat((flat + 1) % total)
    previous = of_flat((flat + total - 1) % total)
    partner = (s, x * 2 + 1 - core)
    second_next = of_flat((flat + 2) % total)
    second_previous = of_flat((flat + total - 2) % total)
    beyond = of_flat((flat + total + 2 - 4 * core) % total)
    def hops(i, ring):
        return min(i, ring - i)

    steps = sorted(range(1, nz), key=lambda i: -hops(i, nz))
    line = [(((z + i) % nz) * ny + y, g) for i in steps]
    across = [(((z + i) % nz) * ny + y, x * 2 + 1 - core) for i in steps]
    offsets = [(i, j) for i in range(ny) for j in range(nx) if i or j]
    offsets = sorted(offsets, key=lambda o: -hops(o[0], ny) - hops(o[1], nx))
    rings = [hops(i, ny) + hops(j, nx) for i, j in offsets]
    plane = [(z * ny + (y + i) % ny, ((x + j) % nx) * 2 + core) for i, j in offsets]
    slot = y * nx + x

    def to(src, dst, send, recv, device):
        return pltpu.make_async_remote_copy(
            src_ref=src, dst_ref=dst, send_sem=send, recv_sem=recv,
            device_id=device, device_id_type=pl.DeviceIdType.MESH,
        )

    def tell(semaphore, device):
        pl.semaphore_signal(
            semaphore, inc=1, device_id=device, device_id_type=pl.DeviceIdType.MESH
        )

    gat2[...] = jnp.zeros_like(gat2)
    for end in (0, coa.shape[0] - 1):
        coa[end] = jnp.zeros(coa.shape[1:], F32)
    barrier = pltpu.get_barrier_semaphore()
    everyone = [*plane, *line, *across, following, previous, partner, second_next, second_previous]
    for device in everyone:
        tell(barrier, device)
    loads = [
        pltpu.make_async_copy(mat_h, mat, local_sem.at[0]),
        pltpu.make_async_copy(rig_h, rigt, local_sem.at[1]),
        pltpu.make_async_copy(res_h, resf.at[pl.ds(1, count)], local_sem.at[2]),
        pltpu.make_async_copy(old_h, oldf.at[pl.ds(1, count)], local_sem.at[3]),
        pltpu.make_async_copy(coa_h, coa.at[pl.ds(1, own_rows // 8)], local_sem.at[4]),
        pltpu.make_async_copy(fac_h, fac, local_sem.at[5]),
        pltpu.make_async_copy(onorm_h, onorm, local_sem.at[6]),
    ]
    for load in loads:
        load.start()
    ubig[...] = jnp.zeros_like(ubig)
    lin[...] = jnp.zeros_like(lin)
    rig[:, ranks:, :] = jnp.zeros((count, 8 - ranks, width), F32)

    loads[0].wait()
    unknowns = lax.broadcasted_iota(jnp.int32, (half, half), 0)
    for q in range(count):
        table[q] = jnp.where(unknowns == mat[pl.ds(q, 1), :], -1.0, 0.0).astype(BF16)
    loads[1].wait()
    for q in range(count):
        for m in range(ranks):
            rig[q, m : m + 1, :] = rigt[m, q : q + 1, :]
    for q in range(count):
        left = rig[q, :, :half]
        high = left.astype(BF16).astype(F32)
        mid = (left - high).astype(BF16).astype(F32)
        parts = jnp.concatenate([high, mid, left - high - mid], 0).astype(BF16)
        moved = mm(parts, table[q], NT)
        nr[q] = moved[:8] + moved[8:16] + moved[16:]

    rows = lax.broadcasted_iota(jnp.int32, (count * 8, LANES), 0)
    chunk = lax.broadcasted_iota(jnp.int32, (count * 8, LANES), 1) // cases
    loads[2].wait()
    resf[count] = jnp.where(is_last, 0.0, resf[count])
    rights = rig[:, :, half:].reshape(count * 8, half)
    lefts = nr[1:count].reshape((count - 1) * 8, half)
    own = resf[1:].reshape(count * cases, half)
    sums = mm(rights, own, NT, HIGHEST)
    before = mm(lefts, own, NT, HIGHEST)
    before = pltpu.roll(before, cases, 1)
    before = jnp.concatenate([jnp.zeros((8, LANES), F32), before], 0)
    sums = jnp.where(rows // 8 == chunk, sums + before, 0.0)
    sums = sums + pltpu.roll(sums, LANES // 2, 1)
    sums = sums + pltpu.roll(sums, LANES // 4, 1)
    for q in range(count):
        m24[q * ranks : (q + 1) * ranks, :] = sums[q * 8 : q * 8 + ranks]
    chunk = chunk[:8]
    tile = jnp.zeros((8, LANES), F32)
    for w in range(own_rows // 8):
        tile = jnp.where(chunk == w, m24[w * 8 : (w + 1) * 8, :], tile)
    faces = jnp.concatenate([pair(resf[count]), jnp.zeros((LANES - 2 * cases, half), BF16)], 0)
    zb[z] = tile
    loads[4].wait()
    firsts, lasts = coa[1], pltpu.roll(coa[coa.shape[0] - 2], ranks, 0)
    rows_in[...] = jnp.where(core == 1, firsts, lasts)
    rows_out[...] = jnp.where(core == 1, lasts, firsts)
    pl.semaphore_wait(barrier, len(everyone))
    edge = core * (coa.shape[0] - 1)
    some = pl.ds(0, ranks)
    halo = [
        to(res_h.at[count - 1], resf.at[0], halo_send.at[0], halo_recv.at[0], following),
        to(nr.at[0], nr.at[count], halo_send.at[1], halo_recv.at[1], previous),
        to(rig.at[count - 1, :, pl.ds(half, half)], rhalo, halo_send.at[2], halo_recv.at[2], following),
        to(old_h.at[count - 1], oldf.at[0], halo_send.at[0], halo_recv.at[0], following),
        to(rows_in.at[some], coa.at[edge, some], halo_send.at[3], halo_recv.at[3], partner),
        to(rows_out.at[some], relay.at[some], halo_send.at[3], halo_recv.at[6], partner),
    ]
    relayed = to(relay.at[some], coa.at[edge, some], halo_send.at[3], halo_recv.at[3], beyond)
    two_faces = to(resf.at[pl.ds(0, 2)], resf.at[pl.ds(0, 2)], halo_send.at[0], halo_recv.at[0], partner)
    two_ends = to(coa.at[pl.ds(0, 2), some], coa.at[pl.ds(0, 2), some], halo_send.at[3], halo_recv.at[3], partner)
    three_ends = to(coa.at[pl.ds(0, 3), some], coa.at[pl.ds(0, 3), some], halo_send.at[3], halo_recv.at[3], partner)

    @pl.when(jnp.logical_not(is_first))
    def _():
        halo[1].start()


    def all_of(ref, number, send, recv):
        whole = ref.at[pl.ds(0, number)]
        return to(whole, whole, send, recv, partner)

    def along_line(ref, at, send, recv, devices):
        for device in devices:
            to(ref.at[at], ref.at[at], send, recv, device).start()
        return all_of(ref, len(devices), send, recv)

    def packed(ref, zl, w):
        block = jnp.zeros((8, LANES), F32)
        for a in range(CHUNKS):
            turned = ref[a * per_chunk + zl]
            if a != w:
                turned = pltpu.roll(turned, ((a - w) * cases) % LANES, 1)
            block = jnp.where(chunk == a, turned, block)
        return block

    def to_plane(ref, depth, send, recv, turn_send, turn_recv):
        def block(yx):
            return ref.at[:, yx, core, pl.ds(0, depth)]

        for device, ring in zip(plane, rings):
            to(block(slot), block(slot), send, recv.at[ring - 1], device).start()
        to(block(slot), block(slot), turn_send, turn_recv, partner).start()

        def turn():
            for ring in sorted(set(rings)):
                members = [o for o, r in zip(offsets, rings) if r == ring]
                group = ref.at[:, pl.ds(0, len(members)), 0, pl.ds(0, depth)]
                to(group, group, send, recv.at[ring - 1], partner).wait_recv()
                for dy, dx in members:
                    theirs = block(((y + ny - dy) % ny) * nx + (x + nx - dx) % nx)
                    to(theirs, theirs, turn_send, turn_recv, partner).start()

        sent = ref.at[:, pl.ds(0, len(plane)), 0, pl.ds(0, depth)]
        both = ref.at[:, :, 0, pl.ds(0, depth)]
        return to(sent, sent, send, recv.at[0], partner), to(both, both, turn_send, turn_recv, partner), turn

    z_copies = along_line(zb, z, z_send, z_recv, line)
    for i in (5, 0, 3, 2, 4):
        halo[i].start()

    block = width // 4

    def forward(left, right, q):
        pairs = jnp.concatenate([mm(pair(left), table[q]).astype(BF16), pair(right)], 1)
        return jnp.concatenate(
            [
                joined(mm(pairs[:, : (i + 1) * block],
                          fac[q, i * block : (i + 1) * block, : (i + 1) * block], NT))
                for i in range(4)
            ], 1,
        )

    def backward(inner, q):
        pairs = pair(inner)
        solved = jnp.concatenate(
            [
                joined(mm(pairs[:, j * block :], fac[q, j * block :, j * block : (j + 1) * block]))
                for j in range(4)
            ], 1,
        )
        returned = joined(mm(pair(solved[:, :half]), table[q], NT))
        return solved[:, half:], returned

    def place(f, above):
        top = (2 + ranks * f if f else 0) if above else 2 + ranks * (f + 1)
        rows_of = (rhalo[:ranks] if f == 0 else rig[f - 1, :ranks, half:]) if above else nr[f, :ranks]
        if f in (0, count):
            rows_of = jnp.where(is_last if f else is_first, 0.0, rows_of)
        ubig[top : top + ranks, f * half : (f + 1) * half] = rows_of

    def keep(rows_of, values, columns):
        high = values.astype(BF16)
        low = (values - high.astype(F32)).astype(BF16)
        lin[rows_of[0] : rows_of[1], columns] = high
        lin[rows_of[0] + taken : rows_of[1] + taken, columns] = high
        lin[rows_of[0] + 2 * taken : rows_of[1] + 2 * taken, columns] = low

    def apply_all(q):
        low_row = (2 + ranks * q) // 8 * 8
        high_row = -(-(2 + ranks * (q + 3)) // 8) * 8
        sides = [
            jnp.concatenate(
                [oldf[f], resf[f], ubig[low_row:high_row, f * half : (f + 1) * half]], 0
            )
            for f in (q, q + 1)
        ]
        inner = forward(*sides, q)
        inner_o[q] = inner[:cases]
        inner_m[q] = inner[cases : 2 * cases]
        start = count * half + q * width
        keep((low_row, high_row), inner[2 * cases :], slice(start, start + width))

    for f in range(count + 1):
        if f > 0:
            place(f, True)
        if f < count:
            place(f, False)
    loads[3].wait()
    oldf[count] = jnp.where(is_last, 0.0, oldf[count])
    loads[5].wait()
    apply_all(1)
    halo[5].wait_recv()
    relayed.start()
    for q in range(2, count - 1):
        apply_all(q)

    def send_corrections():
        @pl.when(jnp.logical_not(is_last))
        def _():
            halo[1].wait_recv()

        added = mm(pair(jnp.where(is_last, 0.0, nr[count])), faces, NT)
        added = added[:8] + pltpu.roll(added[:8], LANES - cases, 1) + added[8:]
        zb2[z] = jnp.where(chunk == 0, added, 0.0)
        for device in line:
            to(zb2.at[z], zb2.at[z], z2_send, z2_recv, device).start()

    far_next = jnp.logical_and(jnp.logical_and(x == nx - 1, y == ny - 1), core == 1)
    pl.when(jnp.logical_not(far_next))(send_corrections)
    z_copies.wait()
    for zl in range(per_chunk):
        for w in range(own_rows // 8):
            gat[zl, slot, core, w * 8 : (w + 1) * 8, :] = packed(zb, zl, w)
    y_copies, c_copies, turn = to_plane(gat, own_rows, y_send, y_recv, c_send, c_recv)
    pl.when(far_next)(send_corrections)
    def take_back(q):
        solved, returned = backward(inner_o[q], q)
        w_o[q] = solved if q else solved + w_o[0]
        if q == 1:
            w_o[0] = returned
        elif q:
            w_o[q - 1] += returned
        else:
            ret_o[...] = returned

    for q in range(1, count - 1):
        take_back(q)
    all_of(zb2, len(line), z2_send, z2_recv).wait()
    for zl in range(per_chunk):
        gat2[zl, slot, core, :ranks] = packed(zb2, zl, 0)[:ranks]
    y2_copies, c2_copies, turn2 = to_plane(gat2, ranks, y2_send, y2_recv, c2_send, c2_recv)
    two_faces.wait_recv()
    halo[2].wait_recv()
    resf[0] = jnp.where(is_first, 0.0, resf[0])
    place(0, True)
    place(count, False)
    oldf[0] = jnp.where(is_first, 0.0, oldf[0])
    for q in (0, count - 1):
        apply_all(q)
    keep((0, taken), ubig[:, half:], slice(0, count * half))
    take_back(0)
    ret_o_copy = to(ret_o, face_o, halo_send.at[4], halo_recv.at[4], previous)
    ret_o_copy.start()
    take_back(count - 1)
    turn()
    two_ends.wait_recv()
    period = min(LANES // 8 * own_rows, span)
    kept = period // own_rows * 8
    source = lax.broadcasted_iota(jnp.int32, (period, kept), 0)
    target = lax.broadcasted_iota(jnp.int32, (period, kept), 1)
    chosen = jnp.where(source == target // 8 * own_rows + target % 8, 1.0, 0.0).astype(BF16)
    coarse_rows = coa[...].reshape(taken, CHUNKS * span)
    following_rows = pltpu.roll(coarse_rows, CHUNKS * span - own_rows, 1)
    for a in range(CHUNKS):
        part = slice(a * span, (a + 1) * span)
        rows_of = slice(a * 2 * taken, (a + 1) * 2 * taken)
        cpair[rows_of] = pair(coarse_rows[:, part])
        shifted = pair(following_rows[:, part])
        cpair2[rows_of] = jnp.concatenate(
            [mm(shifted[:, k : k + period], chosen) for k in range(0, span, period)], 1
        ).astype(BF16)

    turn2()
    c_copies.wait_recv()

    def product(rows_of, gathered):
        high = gathered.astype(BF16)
        low = (gathered - high.astype(F32)).astype(BF16)
        both = mm(rows_of[...], jnp.concatenate([high, low], 1))
        return both[:, :LANES] + both[:, LANES:]

    products = product(cpair, gat[...].reshape(span, LANES))
    c2_copies.wait_recv()
    products = products + product(cpair2, gat2[...].reshape(span // own_rows * 8, LANES))
    chunk_all = lax.broadcasted_iota(jnp.int32, (taken, LANES), 1) // cases
    coeffs = jnp.zeros((taken, LANES), F32)
    for a in range(CHUNKS):
        coeffs = jnp.where(chunk_all == a, joined(products[a * 2 * taken : (a + 1) * 2 * taken]), coeffs)
    coeffs = coeffs + pltpu.roll(coeffs, LANES // 2, 1)
    coeffs = coeffs + pltpu.roll(coeffs, LANES // 4, 1)
    high = coeffs.astype(BF16).astype(F32)
    thrice = jnp.concatenate(
        [high, coeffs - high, high, jnp.zeros((LANES - 3 * taken, LANES), F32)], 0
    ).T[:cases].astype(BF16)
    moved = mm(thrice, lin[...])
    norms, pp, po, oo = (jnp.zeros((cases, 1), F32) for _ in range(4))
    inners = []
    for q in range(count):
        part = resf[q + 1] - moved[:, q * half : (q + 1) * half]
        p_out[q] = part
        start = count * half + q * width
        inner = inner_m[q] - moved[:, start : start + width]
        inners.append(inner)
        old_inner = inner_o[q]
        norms = norms + jnp.sum(part * part, 1, keepdims=True)
        pp = pp + jnp.sum(inner * inner, 1, keepdims=True)
        po = po + jnp.sum(inner * old_inner, 1, keepdims=True)
        oo = oo + jnp.sum(old_inner * old_inner, 1, keepdims=True)

    lane = lax.broadcasted_iota(jnp.int32, (cases, LANES), 1)
    square = jnp.zeros((cases, LANES), F32)
    for i, column in enumerate((norms, pp, po, oo)):
        square = jnp.where(lane == i, column, square)
    square = jnp.concatenate([square, jnp.zeros((LANES - cases, LANES), F32)], 0).T
    here = 2 * z + core
    arz[here] = square[0:1] + sum(pltpu.roll(square[i : i + 1], i * cases, 1) for i in range(1, CHUNKS))
    pairs_of = [device for both in zip(line, across) for device in both]
    az_copies = along_line(arz, here, z_send, az_recv, [*pairs_of, partner])

    for q in range(count):
        solved, returned = backward(inners[q], q)
        w_out[q] = solved
        if q:
            w_out[q - 1] += returned
        else:
            ret_p[...] = returned
            ret_p_copy = to(ret_p, face_p, halo_send.at[5], halo_recv.at[5], previous)
            ret_p_copy.start()
    az_copies.wait()
    arp[slot] = sum(arz[i] for i in range(2 * nz))
    ap_copies = along_line(arp, slot, z2_send, ap_recv, plane)
    loads[6].wait()
    ret_o_copy.wait()
    ret_p_copy.wait()
    w_o[count - 1] = jnp.where(is_last, 0.0, w_o[count - 1] + face_o[...])
    w_out[count - 1] = jnp.where(is_last, 0.0, w_out[count - 1] + face_p[...])
    @pl.when(jnp.logical_not(is_first))
    def _():
        halo[1].wait_send()

    for copy in (two_faces, halo[2], three_ends, y_copies, c_copies, y2_copies, c2_copies):
        copy.wait_send()
    ap_copies.wait()
    totals = sum(arp[i] for i in range(ny * nx))
    norm, pure, mixed, old_part = (pltpu.roll(totals, (-i * cases) % LANES, 1) if i else totals for i in range(CHUNKS))
    beta = norm / jnp.concatenate([onorm[...], jnp.ones((1, LANES - cases), F32)], 1)
    curvature = pure + 2.0 * beta * mixed + beta * beta * old_part
    alpha = norm / curvature
    row = lax.broadcasted_iota(jnp.int32, (LANES, LANES), 0)
    square = jnp.where(row == 0, beta, jnp.where(row == 1, alpha, 0.0)).T
    ab_out[0] = jnp.broadcast_to(square[:cases, 0:1], (cases, half))
    ab_out[1] = jnp.broadcast_to(square[:cases, 1:2], (cases, half))
    column = square[:cases, 0:1]
    for q in range(count):
        w_out[q] += column * w_o[q]


def solution(mesh, ny=4):
    nz, nx = mesh.shape["sub"] // ny, mesh.shape["grp"] // 2
    both = ("sub", "grp")

    def on_device(multipliers, residual, old_direction, old_norms, matching, factor_inverse, rigid_modes, coarse_inverse):
        count, cases, half = multipliers.shape
        ranks = rigid_modes.shape[1]
        own_rows = count * ranks
        width = 2 * half
        coarse = coarse_inverse.shape[1]
        field = jax.ShapeDtypeStruct((count, cases, half), F32)
        dma = pltpu.SemaphoreType.DMA
        taken = own_rows + 16
        vmem = pltpu.VMEM
        scratch = [
            vmem((count + 1, cases, half), F32),
            vmem((count + 1, cases, half), F32),
            vmem((1, cases), F32),
            vmem((count, half), jnp.int32),
            vmem((count, width, width), BF16),
            vmem((ranks, count, width), F32),
            vmem((count, 8, width), F32),
            vmem((8, half), F32),
            vmem((count + 1, 8, half), F32),
            vmem((taken // 8, 8, coarse), F32),
            vmem((8, coarse), F32),
            vmem((8, coarse), F32),
            vmem((8, coarse), F32),
            vmem((2 * CHUNKS * taken, coarse // CHUNKS), BF16),
            vmem((2 * CHUNKS * taken, coarse // CHUNKS // own_rows * 8), BF16),
            vmem((count, half, half), BF16),
            vmem((taken, (count + 1) * half), F32),
            vmem((LANES, count * (half + width)), BF16),
            vmem((own_rows, LANES), F32),
            vmem((nz, 8, LANES), F32),
            vmem((nz, 8, LANES), F32),
            vmem((nz // CHUNKS, ny * nx, 2, own_rows, LANES), F32),
            vmem((nz // CHUNKS, ny * nx, 2, 8, LANES), F32),
            vmem((count, cases, width), F32),
            vmem((count, cases, width), F32),
            vmem((count, cases, half), F32),
            vmem((cases, half), F32),
            vmem((cases, half), F32),
            vmem((cases, half), F32),
            vmem((cases, half), F32),
            vmem((2 * nz, 1, LANES), F32),
            vmem((ny * nx, 1, LANES), F32),
            dma((7,)), dma((6,)), dma((7,)),
            dma, dma, dma, dma((ny // 2 + nx // 2,)), dma, dma,
            dma, dma,
            dma, dma, dma, dma((ny // 2 + nx // 2,)), dma, dma,
        ]
        projected, image, steps = pl.pallas_call(
            functools.partial(kernel, (nz, ny, nx)),
            out_shape=(field, field, jax.ShapeDtypeStruct((2, cases, half), F32)),
            in_specs=[pl.BlockSpec(memory_space=pltpu.HBM)] * 7,
            out_specs=(pl.BlockSpec(memory_space=pltpu.VMEM),) * 3,
            scratch_shapes=scratch,
            compiler_params=pltpu.CompilerParams(
                collective_id=0, has_side_effects=True, vmem_limit_bytes=48 << 20
            ),
        )(*(pltpu.with_memory_space_constraint(a, pltpu.HBM) for a in (residual, old_direction, matching, factor_inverse, rigid_modes.transpose(1, 0, 2), coarse_inverse.reshape(own_rows // 8, 8, coarse), old_norms[None])))
        flat = lax.axis_index(both) * count + jnp.arange(count, dtype=jnp.int32)
        retain = (flat != count * lax.axis_size(both) - 1).astype(F32)[:, None, None]
        beta, alpha = steps[0:1], steps[1:2]
        direction = projected + beta * old_direction * retain
        return multipliers + alpha * direction, residual * retain - alpha * image, direction

    fields = P(both, None, None)
    return jax.shard_map(
        on_device,
        mesh=mesh,
        in_specs=(fields, fields, fields, P(), P(both, None), fields, fields, P(both, None)),
        out_specs=(fields, fields, fields),
        check_vma=False,
    )
```
